256 devices in a mesh: section: 32 (over z_hi, y, core), fsdp: 8 (over x, z_lo).
Axes of the slice: x: 4, y: 4, z: 8 (z_hi: 4, z_lo: 2; z = z_hi * 2 + z_lo), core: 2. Of those that a mesh axis runs over, the one named last changes fastest.
Arguments:
- acts: bfloat16 [2, 2048, 4096], P(None, 'fsdp'), may hold values from -6 to 6
- gains: float32 [2, 4096], replicated, may hold values from 0.1 to 1.9
- gate_w: bfloat16 [4096, 28672], P('fsdp', 'section'), may hold values from -0.09375 to 0.09375
- up_w: bfloat16 [4096, 28672], P('fsdp', 'section'), may hold values from -0.09375 to 0.09375
- down_w: bfloat16 [28672, 4096], P('section', 'fsdp'), may hold values from -0.046875 to 0.046875
Outputs:
- final_acts: bfloat16 [32, 2048, 4096], P('section', 'fsdp')
The draws below stay inside these ranges and needn't reach their ends.
All inputs are finite; a program needn't handle non-finite values.
Results may differ from the reference program's by a relative error of at most 0.0047.
Values may be sent and summed in bfloat16 or wider, within the bound.
No kernel may reach another device: no remote copies, remote signals or barrier semaphores. Data moves between devices by JAX's collectives and lax.ppermute only.
A program may use at most 128 MiB of HBM per device.

```python
import jax
import jax.numpy as jnp
from jax import lax

D = 4096
F = 14336
LAYERS = 2
GROUP = 16
TOKENS = 2048


def shard_levels(stream_key, dims, shards, least, high):
    level, own = 1.0, jax.random.fold_in(stream_key, 6)
    for dim, parts in shards:
        draws = jnp.exp(jax.random.uniform(jax.random.fold_in(own, dim), (parts,), jnp.float32, least / len(shards), high / len(shards)))
        level = level * jnp.repeat(draws, dims[dim] // parts).reshape([-1 if axis == dim else 1 for axis in range(len(dims))])
    return level


def bell_draw(rng, shape, scale, reach, shards=(), dtype=jnp.bfloat16):
    drawn = scale * jax.random.normal(rng, shape, jnp.float32)
    if shards:
        drawn = drawn * shard_levels(rng, shape, shards, -0.22, 0.18)
    return jnp.clip(drawn, -reach, reach).astype(dtype)


def setup_inputs(seed: int = 0) -> dict:
    arg_keys = jax.random.split(jax.random.key(seed), 6)
    return {
        "acts": bell_draw(arg_keys[0], (LAYERS, TOKENS, D), 1.0, 6.0, ((1, 8),)),
        "gains": jnp.clip(1.0 + 0.18 * jax.random.normal(arg_keys[1], (LAYERS, D), jnp.float32), 0.1, 1.9),
        "gate_w": bell_draw(arg_keys[2], (D, LAYERS * F), D ** -0.5, 0.09375, ((0, 8), (1, 32))),
        "up_w": bell_draw(arg_keys[3], (D, LAYERS * F), D ** -0.5, 0.09375, ((0, 8), (1, 32))),
        "down_w": bell_draw(arg_keys[4], (LAYERS * F, D), F ** -0.5, 0.046875, ((0, 32), (1, 8))),
    }


def layer_block(state, gain, gate_w, up_w, down_w):
    widened = state.astype(jnp.float32)
    meansq = lax.optimization_barrier(jnp.mean(widened * widened, axis=-1, keepdims=True))
    normed = (widened * lax.rsqrt(meansq + 1e-05) * gain.astype(jnp.float32)).astype(jnp.bfloat16)
    gate = jnp.dot(normed, gate_w, preferred_element_type=jnp.float32)
    upper = jnp.dot(normed, up_w, preferred_element_type=jnp.float32)
    hidden = (jax.nn.silu(gate) * upper).astype(jnp.bfloat16)
    return (widened + jnp.dot(hidden, down_w, preferred_element_type=jnp.float32)).astype(jnp.bfloat16)

def reference(acts, gains, gate_w, up_w, down_w):
    blocks = []
    for layer in range(LAYERS):
        first = layer * F
        blocks.append(layer_block(acts[layer], gains[layer], gate_w[:, first:first + F], up_w[:, first:first + F], down_w[first:first + F]))
    stacked = jnp.stack(blocks, axis=0)
    rolled = jnp.roll(stacked, 1, axis=0)
    return jnp.repeat(rolled, GROUP, axis=0)
```

```python
import jax
import jax.numpy as jnp
from jax import lax
from jax.sharding import PartitionSpec as P

AXES = (("layer", 2), ("zh", 2), ("y", 4), ("core", 2), ("x", 4), ("zl", 2))
FIRST = 512
BF16, F32 = jnp.bfloat16, jnp.float32


def decode(index):
    place = {}
    for name, size in reversed(AXES):
        place[name] = index % size
        index //= size
    return place


def encode(place):
    index = 0
    for name, size in AXES:
        index = index * size + place[name] % size
    return index


def send(value, **moves):
    pairs = []
    for index in range(256):
        place = decode(index)
        for name, by in moves.items():
            place[name] += by
        pairs.append((index, encode(place)))
    return lax.ppermute(value, ("section", "fsdp"), pairs)


def pick(value, index, axis):
    return lax.dynamic_index_in_dim(value, index, axis, keepdims=False)


def rolled(value, by, axis):
    size = value.shape[axis]
    return lax.dynamic_slice_in_dim(jnp.concatenate([value, value], axis), by % size, size, axis)


def dot(a, b):
    return jnp.dot(a, b, preferred_element_type=F32)


def gathered(shard):
    left, right, far = send(shard, x=-1), send(shard, x=1), send(shard, x=2)
    return [shard, left, far, right]


def local(acts, gains, gate_w, up_w, down_w):
    section, fsdp = lax.axis_index("section"), lax.axis_index("fsdp")
    layer, y, core = section // 16, section // 2 % 4, section % 2
    x, zl = fsdp // 2, fsdp % 2
    tokens, width = acts.shape[1:]
    slab = gate_w.shape[0]
    half = slab // 2

    chunks = [slice(0, FIRST), slice(FIRST, gate_w.shape[1])]
    panels = [gathered(jnp.concatenate([gate_w[:, c], up_w[:, c]], 1)) for c in chunks]
    down_pair = down_w.reshape(-1, 2, half)
    down_own = jnp.concatenate([pick(down_pair, core, 1), send(pick(down_pair, 1 - core, 1), core=1)], 0)
    down_panel = gathered(down_own)

    widened = pick(acts, layer, 0).astype(F32)
    meansq = jnp.mean(widened * widened, axis=-1, keepdims=True)
    normed = (widened * lax.rsqrt(meansq + 1e-05) * pick(gains, layer, 0)).astype(BF16)
    slabs = normed.reshape(tokens, 4, 2, slab)
    mine, theirs = pick(slabs, zl, 2), pick(slabs, 1 - zl, 2)
    rows = jnp.concatenate([mine, send(theirs, zl=1)], 0)
    rows = rolled(rows, x, 1)

    hidden = []
    for panel, c in zip(panels, chunks):
        both = sum(dot(rows[:, k], panel[k]) for k in range(4))
        own = both[:tokens] + send(both[tokens:].astype(BF16), zl=1).astype(F32)
        count = own.shape[1] // 2
        kept = (jax.nn.silu(own[:, :count]) * own[:, count:]).astype(BF16)
        hidden.append(jnp.concatenate([kept, send(kept, zl=1)], 0))
    hidden = jnp.concatenate(hidden, 1)
    hidden = jnp.concatenate([hidden, send(hidden, core=1)], 1)

    product = jnp.concatenate([dot(hidden, panel) for panel in down_panel], 1)
    quarters = product.reshape(2, 4, tokens // 4, 4 * half)
    low = quarters.astype(BF16)
    total = pick(quarters, y, 1)
    for by in (1, 3, 2):
        total = total + send(pick(low, (y + by) % 4, 1), y=by).astype(F32)
    total = total.astype(BF16)
    sums = [sum(send(total[b], layer=1, zh=a, zl=b).astype(F32) for a in range(2)) for b in range(2)]

    sums = jnp.stack(sums, 1).reshape(tokens // 4, 2, 4, half)
    sums = rolled(rolled(sums, zl, 1), 4 - x, 2).transpose(0, 2, 1, 3)
    residual = pick(pick(acts, 1 - layer, 0).reshape(4, tokens // 4, 4, 2, 2, half), y, 0)
    piece = (pick(residual, core, 3).astype(F32) + sums).astype(BF16)
    pieces = jnp.stack([piece, send(piece, y=-1), send(piece, y=2), send(piece, y=1)], 0)
    pieces = rolled(pieces, 4 - y, 0)
    other = send(pieces, core=1)
    first = jnp.where(core == 0, pieces, other)
    second = jnp.where(core == 0, other, pieces)
    return jnp.stack([first, second], 4).reshape(1, tokens, width)


def solution(mesh):
    in_specs = (
        P(None, "fsdp", None),
        P(),
        P("fsdp", "section"),
        P("fsdp", "section"),
        P("section", "fsdp"),
    )
    out_specs = P("section", "fsdp", None)
    return jax.shard_map(local, mesh=mesh, in_specs=in_specs, out_specs=out_specs, check_vma=False)
```

```python
import jax
import jax.numpy as jnp
from jax import lax
from jax.experimental import pallas as pl
from jax.experimental.pallas import tpu as pltpu
from jax.sharding import PartitionSpec as P

AXES = (("layer", 2), ("zh", 2), ("y", 4), ("core", 2), ("x", 4), ("zl", 2))
FIRST = 512
BF16, F32 = jnp.bfloat16, jnp.float32
ROOM = pltpu.CompilerParams(vmem_limit_bytes=40 << 20)


def decode(index):
    place = {}
    for name, size in reversed(AXES):
        place[name] = index % size
        index //= size
    return place


def encode(place):
    index = 0
    for name, size in AXES:
        index = index * size + place[name] % size
    return index


def send(value, **moves):
    pairs = []
    for index in range(256):
        place = decode(index)
        for name, by in moves.items():
            place[name] += by
        pairs.append((index, encode(place)))
    return lax.ppermute(value, ("section", "fsdp"), pairs)


def after(value, *others):
    return lax.optimization_barrier((value, *others))[0]


def dot(a, b):
    return jnp.dot(a, b, preferred_element_type=F32)


def silu(v):
    return v / (1 + jnp.exp(-v))


def gathered(shard, before=None):
    left, far, right = (after(shard, b) for b in before[1:]) if before else (shard,) * 3
    return [shard, send(left, x=-1), send(far, x=2), send(right, x=1)]


def column(place, k, b, size):
    return pl.multiple_of((lax.rem(place[3] + k, 4) * 2 + lax.rem(place[4] + b, 2)) * size, size)


def norm_kernel(place, acts, gains, mine, theirs, normed):
    size = mine.shape[2]
    widened = acts[0].astype(F32)
    meansq = jnp.mean(widened * widened, axis=-1, keepdims=True)
    normed[...] = (widened * lax.rsqrt(meansq + 1e-05) * gains[pl.ds(place[0], 1), :]).astype(BF16)
    for k in range(4):
        mine[k] = normed[:, pl.ds(column(place, k, 0, size), size)]
        theirs[k] = normed[:, pl.ds(column(place, k, 1, size), size)]


def normed_slabs(place, acts, gains, slab):
    tokens, width = acts.shape[1:]
    part = tokens // 4
    shape = jax.ShapeDtypeStruct((4, tokens, slab), BF16)
    spec = pl.BlockSpec((4, part, slab), lambda i, place: (0, i, 0))
    return pl.pallas_call(
        norm_kernel,
        grid_spec=pltpu.PrefetchScalarGridSpec(
            num_scalar_prefetch=1,
            grid=(4,),
            in_specs=[
                pl.BlockSpec((1, part, width), lambda i, place: (place[0], lax.rem(place[1] + i, 4), 0)),
                pl.BlockSpec(gains.shape, lambda i, place: (0, 0)),
            ],
            out_specs=[spec, spec],
            scratch_shapes=[pltpu.VMEM((part, width), BF16)],
        ),
        out_shape=[shape, shape],
        compiler_params=ROOM,
    )(place, acts, gains)


def down_kernel(*refs):
    count = (len(refs) - 4) // 2
    mine, other, near, far = refs[0], refs[1], refs[2:2 + count], refs[2 + count:2 + 2 * count]
    kept, sent = refs[-2:]
    part, size = kept.shape[0], near[0].shape[1]
    for k in range(count):
        product = dot(mine[...], near[k][...]) + dot(other[...], far[k][...])
        columns = slice(k * size, (k + 1) * size)
        kept[:, columns] = product[:part]
        for j in range(3):
            sent[j, :, columns] = product[(j + 1) * part:(j + 2) * part].astype(BF16)


def down_product(mine, other, near, far):
    part, size = mine.shape[0] // 4, near[0].shape[1] * len(near)
    vmem = pl.BlockSpec(memory_space=pltpu.VMEM)
    return pl.pallas_call(
        down_kernel,
        in_specs=[vmem] * (2 + 2 * len(near)),
        out_specs=[vmem, vmem],
        out_shape=[jax.ShapeDtypeStruct((part, size), F32), jax.ShapeDtypeStruct((3, part, size), BF16)],
        compiler_params=ROOM,
    )(mine, other, *near, *far)


def residual_kernel(place, acts, *refs):
    out = refs[-1]
    for b in range(2):
        size = refs[0].shape[1] // 4
        for k in range(4):
            columns = slice(k * size, (k + 1) * size)
            first = pl.multiple_of(column(place, k, b, 2 * size) + place[2] * size, size)
            total = acts[0, :, pl.ds(first, size)].astype(F32) + refs[2 * b][:, columns].astype(F32) + refs[2 * b + 1][:, columns].astype(F32)
            out[:, (4 * b + k) * size:(4 * b + k + 1) * size] = total.astype(BF16)


def with_residual(place, acts, sums):
    part, size = sums[0].shape
    block = pl.BlockSpec((part, size), lambda i, place: (0, 0))
    return pl.pallas_call(
        residual_kernel,
        grid_spec=pltpu.PrefetchScalarGridSpec(
            num_scalar_prefetch=1,
            grid=(1,),
            in_specs=[pl.BlockSpec((1, part, acts.shape[2]), lambda i, place: (1 - place[0], place[1], 0))] + [block] * 4,
            out_specs=pl.BlockSpec((part, 2 * size), lambda i, place: (0, 0)),
        ),
        out_shape=jax.ShapeDtypeStruct((part, 2 * size), BF16),
        compiler_params=ROOM,
    )(place, acts, *sums)


def assembly_kernel(place, *refs):
    out = refs[-1]
    size = refs[0].shape[1] // 8
    for j in range(4):

        @pl.when(pl.program_id(0) == j)
        def _():
            for i in range(2):
                for b in range(2):
                    for k in range(4):
                        first = pl.multiple_of(column(place, k, b, 2 * size) + lax.rem(place[2] + i, 2) * size, size)
                        out[0, :, pl.ds(first, size)] = refs[4 * i + j][:, (4 * b + k) * size:(4 * b + k + 1) * size]


def assembled(place, pieces):
    part, size = pieces[0].shape
    return pl.pallas_call(
        assembly_kernel,
        grid_spec=pltpu.PrefetchScalarGridSpec(
            num_scalar_prefetch=1,
            grid=(4,),
            in_specs=[pl.BlockSpec((part, size), lambda i, place: (0, 0))] * 8,
            out_specs=pl.BlockSpec((1, part, 2 * size), lambda i, place: (0, lax.rem(place[1] + i, 4), 0)),
        ),
        out_shape=jax.ShapeDtypeStruct((1, 4 * part, 2 * size), BF16),
        compiler_params=ROOM,
    )(place, *pieces)


def local(acts, gains, gate_w, up_w, down_w):
    section, fsdp = lax.axis_index("section"), lax.axis_index("fsdp")
    core = section % 2
    place = jnp.stack([section // 16, section // 2 % 4, core, fsdp // 2, fsdp % 2]).astype(jnp.int32)
    tokens = acts.shape[1]
    slab = gate_w.shape[0]
    part = tokens // 4

    gate_panel = gathered(gate_w)
    first_panel = gathered(up_w[:, :FIRST], gate_panel)
    second_panel = gathered(up_w[:, FIRST:], first_panel)
    halves = down_w.reshape(-1, 2, slab // 2)
    near_panel = gathered(lax.dynamic_index_in_dim(halves, core, 1, keepdims=False), second_panel)
    far_panel = gathered(send(lax.dynamic_index_in_dim(halves, 1 - core, 1, keepdims=False), core=1), near_panel)

    mine, theirs = normed_slabs(place, acts, gains, slab)
    got = send(theirs, zl=1)

    def partial_sums(panel):
        own = sum(dot(mine[k], panel[k]) for k in range(4))
        other = sum(dot(got[k], panel[k]) for k in range(4))
        return own + send(other.astype(BF16), zl=1).astype(F32)

    gate, first, second = partial_sums(gate_panel), partial_sums(first_panel), partial_sums(second_panel)
    first = after(first, *second_panel[1:])
    second = after(second, *near_panel[1:])
    kept = [(silu(gate[:, :FIRST]) * first).astype(BF16), (silu(gate[:, FIRST:]) * second).astype(BF16)]
    both = [jnp.stack([h.reshape(4, part, -1), send(h, zl=1).reshape(4, part, -1)], 1).reshape(2 * tokens, -1) for h in kept]
    hidden = jnp.concatenate(both, 1)
    other = send(hidden, core=1)

    total, sent = down_product(hidden, other, near_panel, far_panel)
    for j in (1, 3, 2):
        total = total + send(sent[j - 1], y=j).astype(F32)
    total = total.astype(BF16)
    sums = [send(total[b * part:(b + 1) * part], layer=1, zh=a, zl=b) for b in range(2) for a in range(2)]
    piece = with_residual(place, acts, sums)
    pieces = [piece, send(piece, y=-1), send(piece, y=2), send(piece, y=1)]
    return assembled(place, pieces + [send(p, core=1) for p in pieces])


def solution(mesh):
    in_specs = (
        P(None, "fsdp", None),
        P(),
        P("fsdp", "section"),
        P("fsdp", "section"),
        P("section", "fsdp"),
    )
    out_specs = P("section", "fsdp", None)
    return jax.shard_map(local, mesh=mesh, in_specs=in_specs, out_specs=out_specs, check_vma=False)
```

```python
import jax
import jax.numpy as jnp
from jax import lax
from jax.experimental import pallas as pl
from jax.experimental.pallas import tpu as pltpu
from jax.sharding import PartitionSpec as P

AXES = (("layer", 2), ("zh", 2), ("y", 4), ("core", 2), ("x", 4), ("zl", 2))
FIRST = 512
DEPTH = 3
BF16, F32 = jnp.bfloat16, jnp.float32
ROOM = pltpu.CompilerParams(vmem_limit_bytes=40 << 20)


def decode(index):
    place = {}
    for name, size in reversed(AXES):
        place[name] = index % size
        index //= size
    return place


def encode(place):
    index = 0
    for name, size in AXES:
        index = index * size + place[name] % size
    return index


def send(value, **moves):
    pairs = []
    for index in range(256):
        place = decode(index)
        for name, by in moves.items():
            place[name] += by
        pairs.append((index, encode(place)))
    return lax.ppermute(value, ("section", "fsdp"), pairs)


def after(value, *others):
    return lax.optimization_barrier((value, *others))[0]


def dot(a, b):
    return jnp.dot(a, b, preferred_element_type=F32)


def silu(v):
    return v / (1 + jnp.exp(-v))


def turned(value, way):
    pairs = []
    for index in range(256):
        place = decode(index)
        place["x"] += way * (1 - 2 * place["core"])
        pairs.append((index, encode(place)))
    return lax.ppermute(value, ("section", "fsdp"), pairs)


class Ring:
    def __init__(self):
        self.sent = []

    def turn(self, value, way):
        if len(self.sent) >= DEPTH:
            value = after(value, self.sent[-DEPTH])
        self.sent.append(turned(value, way))
        return self.sent[-1]

    def near(self, shard):
        back = self.turn(shard, 1)
        return [shard, self.turn(shard, -1), None, back]

    def far(self, panel, split):
        panel[2] = (self.turn(panel[3][:split], 1), self.turn(panel[1][split:], -1))


def column(place, core, k, b, size):
    slab = lax.rem(place[3] + k + core * (4 - 2 * k), 4)
    return pl.multiple_of((slab * 2 + lax.rem(place[4] + b, 2)) * size, size)


def norm_kernel(place, acts, gains, mine, theirs, normed):
    size = mine.shape[2]
    widened = acts[0].astype(F32)
    meansq = jnp.mean(widened * widened, axis=-1, keepdims=True)
    normed[...] = (widened * lax.rsqrt(meansq + 1e-05) * gains[pl.ds(place[0], 1), :]).astype(BF16)
    for k in range(4):
        mine[k] = normed[:, pl.ds(column(place, place[2], k, 0, size), size)]
        theirs[k] = normed[:, pl.ds(column(place, place[2], k, 1, size), size)]


def normed_slabs(place, acts, gains, slab):
    tokens, width = acts.shape[1:]
    part = tokens // 4
    shape = jax.ShapeDtypeStruct((4, tokens, slab), BF16)
    spec = pl.BlockSpec((4, part, slab), lambda i, place: (0, i, 0))
    return pl.pallas_call(
        norm_kernel,
        grid_spec=pltpu.PrefetchScalarGridSpec(
            num_scalar_prefetch=1,
            grid=(4,),
            in_specs=[
                pl.BlockSpec((1, part, width), lambda i, place: (place[0], lax.rem(place[1] + i, 4), 0)),
                pl.BlockSpec(gains.shape, lambda i, place: (0, 0)),
            ],
            out_specs=[spec, spec],
            scratch_shapes=[pltpu.VMEM((part, width), BF16)],
        ),
        out_shape=[shape, shape],
        compiler_params=ROOM,
    )(place, acts, gains)


def down_kernel(*refs):
    hidden, panels, (kept, sent) = refs[:2], refs[2:-2], refs[-2:]
    part, size = kept.shape[0], panels[0].shape[1]
    for k in range(4):
        product = 0
        for i in range(2):
            mine = panels[5 * i:5 * i + 5]
            start = 0
            for panel in mine[2:4] if k == 2 else (mine[(0, 1, 2, 4)[k]],):
                stop = start + panel.shape[0]
                product += dot(hidden[i][:, start:stop], panel[...])
                start = stop
        columns = slice(k * size, (k + 1) * size)
        kept[:, columns] = product[:part]
        for j in range(3):
            sent[j, :, columns] = product[(j + 1) * part:(j + 2) * part].astype(BF16)


def down_product(mine, other, near, far):
    part, size = mine.shape[0] // 4, near[0].shape[1] * 4
    vmem = pl.BlockSpec(memory_space=pltpu.VMEM)
    flat = [p for panel in (near, far) for p in (*panel[:2], *panel[2], panel[3])]
    return pl.pallas_call(
        down_kernel,
        in_specs=[vmem] * 12,
        out_specs=[vmem, vmem],
        out_shape=[jax.ShapeDtypeStruct((part, size), F32), jax.ShapeDtypeStruct((3, part, size), BF16)],
        compiler_params=ROOM,
    )(mine, other, *flat)


def residual_kernel(place, acts, *refs):
    out = refs[-1]
    for b in range(2):
        size = refs[0].shape[1] // 4
        for k in range(4):
            columns = slice(k * size, (k + 1) * size)
            first = pl.multiple_of(column(place, place[2], k, b, 2 * size) + place[2] * size, size)
            total = acts[0, :, pl.ds(first, size)].astype(F32) + refs[2 * b][:, columns].astype(F32) + refs[2 * b + 1][:, columns].astype(F32)
            out[:, (4 * b + k) * size:(4 * b + k + 1) * size] = total.astype(BF16)


def with_residual(place, acts, sums):
    part, size = sums[0].shape
    block = pl.BlockSpec((part, size), lambda i, place: (0, 0))
    return pl.pallas_call(
        residual_kernel,
        grid_spec=pltpu.PrefetchScalarGridSpec(
            num_scalar_prefetch=1,
            grid=(1,),
            in_specs=[pl.BlockSpec((1, part, acts.shape[2]), lambda i, place: (1 - place[0], place[1], 0))] + [block] * 4,
            out_specs=pl.BlockSpec((part, 2 * size), lambda i, place: (0, 0)),
        ),
        out_shape=jax.ShapeDtypeStruct((part, 2 * size), BF16),
        compiler_params=ROOM,
    )(place, acts, *sums)


def assembly_kernel(place, *refs):
    out = refs[-1]
    size = refs[0].shape[1] // 8
    for j in range(4):

        @pl.when(pl.program_id(0) == j)
        def _():
            for i in range(2):
                for b in range(2):
                    for k in range(4):
                        core = lax.rem(place[2] + i, 2)
                        first = pl.multiple_of(column(place, core, k, b, 2 * size) + core * size, size)
                        out[0, :, pl.ds(first, size)] = refs[4 * i + j][:, (4 * b + k) * size:(4 * b + k + 1) * size]


def assembled(place, pieces):
    part, size = pieces[0].shape
    return pl.pallas_call(
        assembly_kernel,
        grid_spec=pltpu.PrefetchScalarGridSpec(
            num_scalar_prefetch=1,
            grid=(4,),
            in_specs=[pl.BlockSpec((part, size), lambda i, place: (0, 0))] * 8,
            out_specs=pl.BlockSpec((1, part, 2 * size), lambda i, place: (0, lax.rem(place[1] + i, 4), 0)),
        ),
        out_shape=jax.ShapeDtypeStruct((1, 4 * part, 2 * size), BF16),
        compiler_params=ROOM,
    )(place, *pieces)


def local(acts, gains, gate_w, up_w, down_w):
    section, fsdp = lax.axis_index("section"), lax.axis_index("fsdp")
    core = section % 2
    place = jnp.stack([section // 16, section // 2 % 4, core, fsdp // 2, fsdp % 2]).astype(jnp.int32)
    tokens = acts.shape[1]
    slab = gate_w.shape[0]
    part = tokens // 4

    low, high = down_w[:, :slab // 2], down_w[:, slab // 2:]
    near_own = jnp.where(core == 0, low, high)
    far_own = send(jnp.where(core == 0, high, low), core=1)
    ring = Ring()
    gate_panel = ring.near(gate_w)
    first_panel = ring.near(up_w[:, :FIRST])
    ring.far(gate_panel, slab // 2)
    second_panel = ring.near(after(up_w[:, FIRST:], far_own))
    ring.far(first_panel, slab // 2)
    ring.far(second_panel, slab // 2)
    near_panel = ring.near(near_own)
    far_panel = ring.near(far_own)
    ring.far(near_panel, FIRST)
    ring.far(far_panel, FIRST)

    mine, theirs = normed_slabs(place, acts, gains, slab)
    got = send(theirs, zl=1)

    def partial_sums(panel):
        def product(rows):
            near = sum(dot(rows[k], panel[k]) for k in (0, 1, 3))
            return near + dot(rows[2, :, :slab // 2], panel[2][0]) + dot(rows[2, :, slab // 2:], panel[2][1])

        own, other = product(mine), product(got)
        return own + send(other.astype(BF16), zl=1).astype(F32)

    gate, first, second = partial_sums(gate_panel), partial_sums(first_panel), partial_sums(second_panel)
    first = after(first, second_panel[1], second_panel[3])
    second = after(second, near_panel[1], near_panel[3])
    kept = [(silu(gate[:, :FIRST]) * first).astype(BF16), (silu(gate[:, FIRST:]) * second).astype(BF16)]
    both = [jnp.stack([h.reshape(4, part, -1), send(h, zl=1).reshape(4, part, -1)], 1).reshape(2 * tokens, -1) for h in kept]
    hidden = jnp.concatenate(both, 1)
    other = send(after(hidden, far_panel[1], far_panel[3]), core=1)

    total, sent = down_product(hidden, other, near_panel, far_panel)
    for j in (1, 3, 2):
        total = total + send(sent[j - 1], y=j).astype(F32)
    total = total.astype(BF16)
    sums = [send(total[b * part:(b + 1) * part], layer=1, zh=a, zl=b) for b in range(2) for a in range(2)]
    piece = with_residual(place, acts, sums)
    pieces = [piece, send(piece, y=-1), send(piece, y=2), send(piece, y=1)]
    return assembled(place, pieces + [send(p, core=1) for p in pieces])


def solution(mesh):
    in_specs = (
        P(None, "fsdp", None),
        P(),
        P("fsdp", "section"),
        P("fsdp", "section"),
        P("section", "fsdp"),
    )
    out_specs = P("section", "fsdp", None)
    return jax.shard_map(local, mesh=mesh, in_specs=in_specs, out_specs=out_specs, check_vma=False)
```

```python
import functools

import jax
import jax.numpy as jnp
from jax import lax
from jax.experimental import pallas as pl
from jax.experimental.pallas import tpu as pltpu
from jax.sharding import PartitionSpec as P

AXES = (("layer", 2), ("zh", 2), ("y", 4), ("core", 2), ("x", 4), ("zl", 2))
FIRST = 512
DEPTH = 3
CHUNKS = ((0, 3), (1, 2))
BF16, F32 = jnp.bfloat16, jnp.float32
ROOM = pltpu.CompilerParams(vmem_limit_bytes=40 << 20)


def decode(index):
    place = {}
    for name, size in reversed(AXES):
        place[name] = index % size
        index //= size
    return place


def encode(place):
    index = 0
    for name, size in AXES:
        index = index * size + place[name] % size
    return index


def send(value, **moves):
    pairs = []
    for index in range(256):
        place = decode(index)
        for name, by in moves.items():
            place[name] += by
        pairs.append((index, encode(place)))
    return lax.ppermute(value, ("section", "fsdp"), pairs)


def after(value, *others):
    return lax.optimization_barrier((value, *others))[0]


def dot(a, b):
    return jnp.dot(a, b, preferred_element_type=F32)


def silu(v):
    return v / (1 + jnp.exp(-v))


def turned(value, way):
    pairs = []
    for index in range(256):
        place = decode(index)
        place["x"] += way * (1 - 2 * place["core"])
        pairs.append((index, encode(place)))
    return lax.ppermute(value, ("section", "fsdp"), pairs)


class Ring:
    def __init__(self):
        self.sent = []

    def turn(self, value, way):
        if len(self.sent) >= DEPTH:
            value = after(value, self.sent[-DEPTH])
        self.sent.append(turned(value, way))
        return self.sent[-1]

    def near(self, shard):
        back = self.turn(shard, 1)
        return [shard, self.turn(shard, -1), None, back]

    def far(self, panel, split):
        panel[2] = (self.turn(panel[3][:split], 1), self.turn(panel[1][split:], -1))


def column(place, core, k, b, size):
    slab = lax.rem(place[3] + k + core * (4 - 2 * k), 4)
    return pl.multiple_of((slab * 2 + lax.rem(place[4] + b, 2)) * size, size)


def norm_kernel(place, acts, gains, mine, theirs, normed):
    size = mine.shape[2]
    widened = acts[0].astype(F32)
    meansq = jnp.mean(widened * widened, axis=-1, keepdims=True)
    normed[...] = (widened * lax.rsqrt(meansq + 1e-05) * gains[pl.ds(place[0], 1), :]).astype(BF16)
    for k in range(4):
        mine[k] = normed[:, pl.ds(column(place, place[2], k, 0, size), size)]
        theirs[k] = normed[:, pl.ds(column(place, place[2], k, 1, size), size)]


def normed_slabs(place, acts, gains, slab):
    tokens, width = acts.shape[1:]
    part = tokens // 4
    shape = jax.ShapeDtypeStruct((4, tokens, slab), BF16)
    spec = pl.BlockSpec((4, part, slab), lambda i, place: (0, i, 0))
    return pl.pallas_call(
        norm_kernel,
        grid_spec=pltpu.PrefetchScalarGridSpec(
            num_scalar_prefetch=1,
            grid=(4,),
            in_specs=[
                pl.BlockSpec((1, part, width), lambda i, place: (place[0], lax.rem(place[1] + i, 4), 0)),
                pl.BlockSpec(gains.shape, lambda i, place: (0, 0)),
            ],
            out_specs=[spec, spec],
            scratch_shapes=[pltpu.VMEM((part, width), BF16)],
        ),
        out_shape=[shape, shape],
        compiler_params=ROOM,
    )(place, acts, gains)


def down_kernel(*refs):
    hidden, panels, (kept, sent) = refs[:2], refs[2:-2], refs[-2:]
    part, size = kept.shape[0], panels[0].shape[1]
    for k in range(kept.shape[1] // size):
        product, start = 0, [0, 0]
        while start[1] < hidden[1].shape[1]:
            i = int(start[0] == hidden[0].shape[1])
            stop = start[i] + panels[0].shape[0]
            product += dot(hidden[i][:, start[i]:stop], panels[0][...])
            start[i], panels = stop, panels[1:]
        columns = slice(k * size, (k + 1) * size)
        kept[:, columns] = product[:part]
        for j in range(3):
            sent[j, :, columns] = product[(j + 1) * part:(j + 2) * part].astype(BF16)


def down_product(mine, other, near, far, chunk):
    part, size = mine.shape[0] // 4, near[0].shape[1] * len(chunk)
    vmem = pl.BlockSpec(memory_space=pltpu.VMEM)
    flat = []
    for k in chunk:
        for panel in (near, far):
            flat += panel[k] if k == 2 else [panel[k]]
    return pl.pallas_call(
        down_kernel,
        in_specs=[vmem] * (2 + len(flat)),
        out_specs=[vmem, vmem],
        out_shape=[jax.ShapeDtypeStruct((part, size), F32), jax.ShapeDtypeStruct((3, part, size), BF16)],
        compiler_params=ROOM,
    )(mine, other, *flat)


def residual_kernel(chunk, place, acts, *refs):
    out = refs[-1]
    size = refs[0].shape[1] // len(chunk)
    for b in range(2):
        for i, k in enumerate(chunk):
            columns = slice(i * size, (i + 1) * size)
            first = pl.multiple_of(column(place, place[2], k, b, 2 * size) + place[2] * size, size)
            total = acts[0, :, pl.ds(first, size)].astype(F32) + refs[2 * b][:, columns].astype(F32) + refs[2 * b + 1][:, columns].astype(F32)
            first = (len(chunk) * b + i) * size
            out[:, first:first + size] = total.astype(BF16)


def with_residual(place, acts, sums, chunk):
    part, size = sums[0].shape
    block = pl.BlockSpec((part, size), lambda i, place: (0, 0))
    return pl.pallas_call(
        functools.partial(residual_kernel, chunk),
        grid_spec=pltpu.PrefetchScalarGridSpec(
            num_scalar_prefetch=1,
            grid=(1,),
            in_specs=[pl.BlockSpec((1, part, acts.shape[2]), lambda i, place: (1 - place[0], place[1], 0))] + [block] * 4,
            out_specs=pl.BlockSpec((part, 2 * size), lambda i, place: (0, 0)),
        ),
        out_shape=jax.ShapeDtypeStruct((part, 2 * size), BF16),
        compiler_params=ROOM,
    )(place, acts, *sums)


def assembly_kernel(place, *refs):
    out = refs[-1]
    for j in range(4):

        @pl.when(pl.program_id(0) == j)
        def _():
            for c, chunk in enumerate(CHUNKS):
                for i in range(2):
                    piece = refs[8 * c + 4 * i + j]
                    size = piece.shape[1] // (2 * len(chunk))
                    core = lax.rem(place[2] + i, 2)
                    for b in range(2):
                        for n, k in enumerate(chunk):
                            first = pl.multiple_of(column(place, core, k, b, 2 * size) + core * size, size)
                            start = (len(chunk) * b + n) * size
                            out[0, :, pl.ds(first, size)] = piece[:, start:start + size]


def assembled(place, pieces, width):
    part = pieces[0].shape[0]
    return pl.pallas_call(
        assembly_kernel,
        grid_spec=pltpu.PrefetchScalarGridSpec(
            num_scalar_prefetch=1,
            grid=(4,),
            in_specs=[pl.BlockSpec(p.shape, lambda i, place: (0, 0)) for p in pieces],
            out_specs=pl.BlockSpec((1, part, width), lambda i, place: (0, lax.rem(place[1] + i, 4), 0)),
        ),
        out_shape=jax.ShapeDtypeStruct((1, 4 * part, width), BF16),
        compiler_params=ROOM,
    )(place, *pieces)


def local(acts, gains, gate_w, up_w, down_w):
    section, fsdp = lax.axis_index("section"), lax.axis_index("fsdp")
    core = section % 2
    place = jnp.stack([section // 16, section // 2 % 4, core, fsdp // 2, fsdp % 2]).astype(jnp.int32)
    tokens = acts.shape[1]
    slab = gate_w.shape[0]
    part = tokens // 4

    low, high = down_w[:, :slab // 2], down_w[:, slab // 2:]
    near_own = jnp.where(core == 0, low, high)
    far_own = send(jnp.where(core == 0, high, low), core=1)
    ring = Ring()
    gate_panel = ring.near(gate_w)
    first_panel = ring.near(up_w[:, :FIRST])
    ring.far(gate_panel, slab // 2)
    second_panel = ring.near(after(up_w[:, FIRST:], far_own))
    ring.far(first_panel, slab // 2)
    ring.far(second_panel, slab // 2)
    near_panel = ring.near(near_own)
    far_panel = ring.near(far_own)
    ring.far(near_panel, FIRST)
    ring.far(far_panel, FIRST)

    mine, theirs = normed_slabs(place, acts, gains, slab)
    got = send(theirs, zl=1)

    def partial_sums(panel):
        def product(rows):
            near = sum(dot(rows[k], panel[k]) for k in (0, 1, 3))
            return near + dot(rows[2, :, :slab // 2], panel[2][0]) + dot(rows[2, :, slab // 2:], panel[2][1])

        own, other = product(mine), product(got)
        return own + send(other.astype(BF16), zl=1).astype(F32)

    gate, first, second = partial_sums(gate_panel), partial_sums(first_panel), partial_sums(second_panel)
    first = after(first, second_panel[1], second_panel[3])
    second = after(second, near_panel[1], near_panel[3])
    kept = [(silu(gate[:, :FIRST]) * first).astype(BF16), (silu(gate[:, FIRST:]) * second).astype(BF16)]
    both = [jnp.stack([h.reshape(4, part, -1), send(h, zl=1).reshape(4, part, -1)], 1).reshape(2 * tokens, -1) for h in kept]
    hidden = jnp.concatenate(both, 1)
    other = send(after(hidden, far_panel[1], far_panel[3]), core=1)

    pieces = []
    for chunk in CHUNKS:
        total, sent = down_product(hidden, other, near_panel, far_panel, chunk)
        came = [send(sent[j - 1], y=j) for j in (1, 3, 2)]
        for value in came:
            total = total + value.astype(F32)
        total = total.astype(BF16)
        sums = [send(total[b * part:(b + 1) * part], layer=1, zh=a, zl=b) for b in range(2) for a in range(2)]
        piece = with_residual(place, acts, sums, chunk)
        own = [piece, send(piece, y=-1), send(piece, y=2), send(piece, y=1)]
        pieces += own + [send(p, core=1) for p in own]
        hidden = after(hidden, came[0])
    return assembled(place, pieces, acts.shape[2])


def solution(mesh):
    in_specs = (
        P(None, "fsdp", None),
        P(),
        P("fsdp", "section"),
        P("fsdp", "section"),
        P("section", "fsdp"),
    )
    out_specs = P("section", "fsdp", None)
    return jax.shard_map(local, mesh=mesh, in_specs=in_specs, out_specs=out_specs, check_vma=False)
```

```python
import functools

import jax
import jax.numpy as jnp
from jax import lax
from jax.experimental import pallas as pl
from jax.experimental.pallas import tpu as pltpu
from jax.sharding import PartitionSpec as P

AXES = (("layer", 2), ("zh", 2), ("y", 4), ("core", 2), ("x", 4), ("zl", 2))
FIRST = 640
DEPTH = 3
CHUNKS = ((0, 3), (1, 2))
BF16, F32 = jnp.bfloat16, jnp.float32
ROOM = pltpu.CompilerParams(vmem_limit_bytes=40 << 20)


def decode(index):
    place = {}
    for name, size in reversed(AXES):
        place[name] = index % size
        index //= size
    return place


def encode(place):
    index = 0
    for name, size in AXES:
        index = index * size + place[name] % size
    return index


def send(value, **moves):
    pairs = []
    for index in range(256):
        place = decode(index)
        for name, by in moves.items():
            place[name] += by
        pairs.append((index, encode(place)))
    return lax.ppermute(value, ("section", "fsdp"), pairs)


def after(value, *others):
    return lax.optimization_barrier((value, *others))[0]


def dot(a, b):
    return jnp.dot(a, b, preferred_element_type=F32)


def silu(v):
    return v / (1 + jnp.exp(-v))


def turned(value, way):
    pairs = []
    for index in range(256):
        place = decode(index)
        place["x"] += way * (1 - 2 * place["core"])
        pairs.append((index, encode(place)))
    return lax.ppermute(value, ("section", "fsdp"), pairs)


def crossed(value, a):
    pairs = []
    for index in range(256):
        place = decode(index)
        place["zl"] += place["zh"]
        place["zh"] += a
        place["layer"] += 1
        pairs.append((index, encode(place)))
    return lax.ppermute(value, ("section", "fsdp"), pairs)


class Ring:
    def __init__(self):
        self.sent = []

    def turn(self, value, way):
        if len(self.sent) >= DEPTH:
            value = after(value, self.sent[-DEPTH])
        self.sent.append(turned(value, way))
        return self.sent[-1]

    def near(self, shard):
        back = self.turn(shard, 1)
        return [shard, self.turn(shard, -1), None, back]

    def far(self, panel, split):
        panel[2] = (self.turn(panel[3][:split], 1), self.turn(panel[1][split:], -1))


def column(place, core, k, b, size):
    slab = lax.rem(place[3] + k + core * (4 - 2 * k), 4)
    return pl.multiple_of((slab * 2 + lax.rem(place[4] + b, 2)) * size, size)


def norm_kernel(place, acts, gains, mine, theirs, normed):
    size = mine.shape[2]
    widened = acts[0].astype(F32)
    meansq = jnp.mean(widened * widened, axis=-1, keepdims=True)
    normed[...] = (widened * lax.rsqrt(meansq + 1e-05) * gains[pl.ds(place[0], 1), :]).astype(BF16)
    for k in range(4):
        mine[k] = normed[:, pl.ds(column(place, place[2], k, 0, size), size)]
        theirs[k] = normed[:, pl.ds(column(place, place[2], k, 1, size), size)]


def normed_slabs(place, acts, gains, slab):
    tokens, width = acts.shape[1:]
    part = tokens // 4
    shape = jax.ShapeDtypeStruct((4, tokens, slab), BF16)
    spec = pl.BlockSpec((4, part, slab), lambda i, place: (0, i, 0))
    return pl.pallas_call(
        norm_kernel,
        grid_spec=pltpu.PrefetchScalarGridSpec(
            num_scalar_prefetch=1,
            grid=(4,),
            in_specs=[
                pl.BlockSpec((1, part, width), lambda i, place: (place[0], lax.rem(place[1] + i, 4), 0)),
                pl.BlockSpec(gains.shape, lambda i, place: (0, 0)),
            ],
            out_specs=[spec, spec],
            scratch_shapes=[pltpu.VMEM((part, width), BF16)],
        ),
        out_shape=[shape, shape],
        compiler_params=ROOM,
    )(place, acts, gains)


def down_kernel(chunk, *refs):
    hidden, panels, (kept, sent) = refs[:8], list(refs[8:-2]), refs[-2:]
    size = panels[0].shape[1]
    part = kept.shape[0] // 2
    first = hidden[0].shape[1]
    for n, k in enumerate(chunk):
        rows = []
        for _ in range(2):
            if k == 2:
                rows += [panels.pop(0)[...], panels.pop(0)[...]]
            else:
                panel = panels.pop(0)
                rows += [panel[:first], panel[first:]]
        columns = slice(n * size, (n + 1) * size)
        for b in range(2):
            product = sum(dot(hidden[4 * b + i][...], rows[i]) for i in range(4))
            kept[b * part:(b + 1) * part, columns] = product[:part]
            for j in range(3):
                sent[j, b * part:(b + 1) * part, columns] = product[(j + 1) * part:(j + 2) * part].astype(BF16)


def down_product(hidden, near, far, chunk):
    part, size = hidden[0].shape[0] // 2, near[0].shape[1] * len(chunk)
    vmem = pl.BlockSpec(memory_space=pltpu.VMEM)
    flat = []
    for k in chunk:
        for panel in (near, far):
            flat += panel[k] if k == 2 else [panel[k]]
    return pl.pallas_call(
        functools.partial(down_kernel, chunk),
        in_specs=[vmem] * (8 + len(flat)),
        out_specs=[vmem, vmem],
        out_shape=[jax.ShapeDtypeStruct((part, size), F32), jax.ShapeDtypeStruct((3, part, size), BF16)],
        compiler_params=ROOM,
    )(*hidden, *flat)


def residual_kernel(chunk, place, acts, *refs):
    out = refs[-1]
    size = refs[0].shape[1] // len(chunk)
    for a in range(2):
        for i, k in enumerate(chunk):
            first = pl.multiple_of(column(place, place[2], k, place[5] + a, 2 * size) + place[2] * size, size)
            total = acts[0, :, pl.ds(first, size)].astype(F32) + refs[a][:, i * size:(i + 1) * size].astype(F32)
            first = (len(chunk) * a + i) * size
            out[:, first:first + size] = total.astype(BF16)


def with_residual(place, acts, sums, chunk):
    part, size = sums[0].shape
    block = pl.BlockSpec((part, size), lambda i, place: (0, 0))
    return pl.pallas_call(
        functools.partial(residual_kernel, chunk),
        grid_spec=pltpu.PrefetchScalarGridSpec(
            num_scalar_prefetch=1,
            grid=(1,),
            in_specs=[pl.BlockSpec((1, part, acts.shape[2]), lambda i, place: (1 - place[0], place[1], 0))] + [block] * 2,
            out_specs=pl.BlockSpec((part, 2 * size), lambda i, place: (0, 0)),
        ),
        out_shape=jax.ShapeDtypeStruct((part, 2 * size), BF16),
        compiler_params=ROOM,
    )(place, acts, *sums)


def assembly_kernel(place, *refs):
    out = refs[-1]
    for j in range(4):

        @pl.when(pl.program_id(0) == j)
        def _():
            for c, chunk in enumerate(CHUNKS):
                for i in range(2):
                    piece = refs[8 * c + 4 * i + j]
                    size = piece.shape[1] // (2 * len(chunk))
                    core = lax.rem(place[2] + i, 2)
                    for a in range(2):
                        for n, k in enumerate(chunk):
                            first = pl.multiple_of(column(place, core, k, place[5] + a, 2 * size) + core * size, size)
                            start = (len(chunk) * a + n) * size
                            out[0, :, pl.ds(first, size)] = piece[:, start:start + size]


def assembled(place, pieces, width):
    part = pieces[0].shape[0]
    return pl.pallas_call(
        assembly_kernel,
        grid_spec=pltpu.PrefetchScalarGridSpec(
            num_scalar_prefetch=1,
            grid=(4,),
            in_specs=[pl.BlockSpec(p.shape, lambda i, place: (0, 0)) for p in pieces],
            out_specs=pl.BlockSpec((1, part, width), lambda i, place: (0, lax.rem(place[1] + i, 4), 0)),
        ),
        out_shape=jax.ShapeDtypeStruct((1, 4 * part, width), BF16),
        compiler_params=ROOM,
    )(place, *pieces)


def local(acts, gains, gate_w, up_w, down_w):
    section, fsdp = lax.axis_index("section"), lax.axis_index("fsdp")
    core, zh = section % 2, section // 8 % 2
    place = jnp.stack([section // 16, section // 2 % 4, core, fsdp // 2, fsdp % 2, zh]).astype(jnp.int32)
    tokens = acts.shape[1]
    slab = gate_w.shape[0]
    part = tokens // 4

    low, high = down_w[:, :slab // 2], down_w[:, slab // 2:]
    near_own = jnp.where(core == 0, low, high)
    far_own = send(jnp.where(core == 0, high, low), core=1)
    ring = Ring()
    gate_panel = ring.near(gate_w)
    first_panel = ring.near(up_w[:, :FIRST])
    ring.far(gate_panel, slab // 2)
    near_panel = ring.near(after(near_own, far_own))
    ring.far(first_panel, slab // 2)
    second_panel = ring.near(up_w[:, FIRST:])
    ring.far(near_panel, FIRST)
    ring.far(second_panel, slab // 2)
    far_panel = ring.near(far_own)
    ring.far(far_panel, FIRST)

    mine, theirs = normed_slabs(place, acts, gains, slab)
    got = send(theirs, zl=1)

    def partial_sums(panel):
        def product(rows):
            near = sum(dot(rows[k], panel[k]) for k in (0, 1, 3))
            return near + dot(rows[2, :, :slab // 2], panel[2][0]) + dot(rows[2, :, slab // 2:], panel[2][1])

        own, other = product(mine), product(got)
        return own + send(other.astype(BF16), zl=1).astype(F32)

    gate, first, second = partial_sums(gate_panel), partial_sums(first_panel), partial_sums(second_panel)
    kept = [(silu(gate[:, :FIRST]) * first).astype(BF16), (silu(gate[:, FIRST:]) * second).astype(BF16)]
    theirs = [send(h, zl=1) for h in kept]
    theirs[1] = after(theirs[1], far_panel[1], far_panel[3])
    hidden = []
    for pair in (kept, theirs):
        hidden += pair + [send(h, core=1) for h in pair]

    pieces = []
    for chunk in CHUNKS:
        total, sent = down_product(hidden, near_panel, far_panel, chunk)
        came = [send(sent[j - 1], y=j) for j in (1, 3, 2)]
        for value in came:
            total = total + value.astype(F32)
        low, high = total[:part], total[part:]
        away = jnp.where(zh == 0, high, low).astype(BF16)
        total = (jnp.where(zh == 0, low, high) + send(away, zh=1).astype(F32)).astype(BF16)
        piece = with_residual(place, acts, [crossed(total, a) for a in range(2)], chunk)
        own = [piece, send(piece, y=-1), send(piece, y=2), send(piece, y=1)]
        pieces += own + [send(p, core=1) for p in own]
        hidden[0] = after(hidden[0], came[0])
    return assembled(place, pieces, acts.shape[2])


def solution(mesh):
    in_specs = (
        P(None, "fsdp", None),
        P(),
        P("fsdp", "section"),
        P("fsdp", "section"),
        P("section", "fsdp"),
    )
    out_specs = P("section", "fsdp", None)
    return jax.shard_map(local, mesh=mesh, in_specs=in_specs, out_specs=out_specs, check_vma=False)
```

```python
import functools

import jax
import jax.numpy as jnp
from jax import lax
from jax.experimental import pallas as pl
from jax.experimental.pallas import tpu as pltpu
from jax.sharding import PartitionSpec as P

AXES = (("layer", 2), ("zh", 2), ("y", 4), ("core", 2), ("x", 4), ("zl", 2))
FIRST = 640
DEPTH = 3
CHUNKS = ((0, 3), (1, 2))
BF16, F32 = jnp.bfloat16, jnp.float32
ROOM = pltpu.CompilerParams(vmem_limit_bytes=40 << 20)


def decode(index):
    place = {}
    for name, size in reversed(AXES):
        place[name] = index % size
        index //= size
    return place


def encode(place):
    index = 0
    for name, size in AXES:
        index = index * size + place[name] % size
    return index


def send(value, **moves):
    pairs = []
    for index in range(256):
        place = decode(index)
        for name, by in moves.items():
            place[name] += by
        pairs.append((index, encode(place)))
    return lax.ppermute(value, ("section", "fsdp"), pairs)


def after(value, *others):
    return lax.optimization_barrier((value, *others))[0]


def dot(a, b):
    return jnp.dot(a, b, preferred_element_type=F32)


def silu(v):
    return v / (1 + jnp.exp(-v))


def turned(value, way):
    pairs = []
    for index in range(256):
        place = decode(index)
        place["x"] += way * (1 - 2 * place["core"])
        pairs.append((index, encode(place)))
    return lax.ppermute(value, ("section", "fsdp"), pairs)


class Ring:
    def __init__(self):
        self.sent = []

    def turn(self, value, way):
        if len(self.sent) >= DEPTH:
            value = after(value, self.sent[-DEPTH])
        self.sent.append(turned(value, way))
        return self.sent[-1]

    def near(self, shard):
        back = self.turn(shard, 1)
        return [shard, self.turn(shard, -1), None, back]

    def far(self, panel, split):
        panel[2] = (self.turn(panel[3][:split], 1), self.turn(panel[1][split:], -1))


def column(place, core, k, b, size):
    slab = lax.rem(place[3] + k + core * (4 - 2 * k), 4)
    return pl.multiple_of((slab * 2 + lax.rem(place[4] + b, 2)) * size, size)


def norm_kernel(place, acts, gains, mine, theirs, normed):
    size = mine.shape[2]
    widened = acts[0].astype(F32)
    meansq = jnp.mean(widened * widened, axis=-1, keepdims=True)
    normed[...] = (widened * lax.rsqrt(meansq + 1e-05) * gains[pl.ds(place[0], 1), :]).astype(BF16)
    for k in range(4):
        mine[k] = normed[:, pl.ds(column(place, place[2], k, 0, size), size)]
        theirs[k] = normed[:, pl.ds(column(place, place[2], k, 1, size), size)]


def normed_slabs(place, acts, gains, slab):
    tokens, width = acts.shape[1:]
    part = tokens // 4
    shape = jax.ShapeDtypeStruct((4, tokens, slab), BF16)
    spec = pl.BlockSpec((4, part, slab), lambda i, place: (0, i, 0))
    return pl.pallas_call(
        norm_kernel,
        grid_spec=pltpu.PrefetchScalarGridSpec(
            num_scalar_prefetch=1,
            grid=(4,),
            in_specs=[
                pl.BlockSpec((1, part, width), lambda i, place: (place[0], lax.rem(place[1] + i, 4), 0)),
                pl.BlockSpec(gains.shape, lambda i, place: (0, 0)),
            ],
            out_specs=[spec, spec],
            scratch_shapes=[pltpu.VMEM((part, width), BF16)],
        ),
        out_shape=[shape, shape],
        compiler_params=ROOM,
    )(place, acts, gains)


def down_kernel(chunk, *refs):
    hidden, panels, (kept, sent) = refs[:8], list(refs[8:-2]), refs[-2:]
    size = panels[0].shape[1]
    part = kept.shape[0] // 2
    first = hidden[0].shape[1]
    for n, k in enumerate(chunk):
        rows = []
        for _ in range(2):
            if k == 2:
                rows += [panels.pop(0)[...], panels.pop(0)[...]]
            else:
                panel = panels.pop(0)
                rows += [panel[:first], panel[first:]]
        columns = slice(n * size, (n + 1) * size)
        for b in range(2):
            product = sum(dot(hidden[4 * b + i][...], rows[i]) for i in range(4))
            kept[b * part:(b + 1) * part, columns] = product[:part]
            for j in range(3):
                sent[j, b * part:(b + 1) * part, columns] = product[(j + 1) * part:(j + 2) * part].astype(BF16)


def down_product(hidden, near, far, chunk):
    part, size = hidden[0].shape[0] // 2, near[0].shape[1] * len(chunk)
    vmem = pl.BlockSpec(memory_space=pltpu.VMEM)
    flat = []
    for k in chunk:
        for panel in (near, far):
            flat += panel[k] if k == 2 else [panel[k]]
    return pl.pallas_call(
        functools.partial(down_kernel, chunk),
        in_specs=[vmem] * (8 + len(flat)),
        out_specs=[vmem, vmem],
        out_shape=[jax.ShapeDtypeStruct((part, size), F32), jax.ShapeDtypeStruct((3, part, size), BF16)],
        compiler_params=ROOM,
    )(*hidden, *flat)


def residual_kernel(chunk, place, acts, *refs):
    out = refs[-1]
    size = refs[0].shape[1] // len(chunk)
    for b in range(2):
        for i, k in enumerate(chunk):
            columns = slice(i * size, (i + 1) * size)
            first = pl.multiple_of(column(place, place[2], k, b, 2 * size) + place[2] * size, size)
            total = acts[0, :, pl.ds(first, size)].astype(F32) + refs[2 * b][:, columns].astype(F32) + refs[2 * b + 1][:, columns].astype(F32)
            first = (len(chunk) * b + i) * size
            out[:, first:first + size] = total.astype(BF16)


def with_residual(place, acts, sums, chunk):
    part, size = sums[0].shape
    block = pl.BlockSpec((part, size), lambda i, place: (0, 0))
    return pl.pallas_call(
        functools.partial(residual_kernel, chunk),
        grid_spec=pltpu.PrefetchScalarGridSpec(
            num_scalar_prefetch=1,
            grid=(1,),
            in_specs=[pl.BlockSpec((1, part, acts.shape[2]), lambda i, place: (1 - place[0], place[1], 0))] + [block] * 4,
            out_specs=pl.BlockSpec((part, 2 * size), lambda i, place: (0, 0)),
        ),
        out_shape=jax.ShapeDtypeStruct((part, 2 * size), BF16),
        compiler_params=ROOM,
    )(place, acts, *sums)


def assembly_kernel(place, *refs):
    out = refs[-1]
    for j in range(4):

        @pl.when(pl.program_id(0) == j)
        def _():
            for c, chunk in enumerate(CHUNKS):
                for i in range(2):
                    piece = refs[8 * c + 4 * i + j]
                    size = piece.shape[1] // (2 * len(chunk))
                    core = lax.rem(place[2] + i, 2)
                    for b in range(2):
                        for n, k in enumerate(chunk):
                            first = pl.multiple_of(column(place, core, k, b, 2 * size) + core * size, size)
                            start = (len(chunk) * b + n) * size
                            out[0, :, pl.ds(first, size)] = piece[:, start:start + size]


def assembled(place, pieces, width):
    part = pieces[0].shape[0]
    return pl.pallas_call(
        assembly_kernel,
        grid_spec=pltpu.PrefetchScalarGridSpec(
            num_scalar_prefetch=1,
            grid=(4,),
            in_specs=[pl.BlockSpec(p.shape, lambda i, place: (0, 0)) for p in pieces],
            out_specs=pl.BlockSpec((1, part, width), lambda i, place: (0, lax.rem(place[1] + i, 4), 0)),
        ),
        out_shape=jax.ShapeDtypeStruct((1, 4 * part, width), BF16),
        compiler_params=ROOM,
    )(place, *pieces)


def local(acts, gains, gate_w, up_w, down_w):
    section, fsdp = lax.axis_index("section"), lax.axis_index("fsdp")
    core = section % 2
    place = jnp.stack([section // 16, section // 2 % 4, core, fsdp // 2, fsdp % 2]).astype(jnp.int32)
    tokens = acts.shape[1]
    slab = gate_w.shape[0]
    part = tokens // 4

    low, high = down_w[:, :slab // 2], down_w[:, slab // 2:]
    near_own = jnp.where(core == 0, low, high)
    far_own = send(jnp.where(core == 0, high, low), core=1)
    ring = Ring()
    gate_panel = ring.near(gate_w)
    first_panel = ring.near(up_w[:, :FIRST])
    ring.far(gate_panel, slab // 2)
    near_panel = ring.near(after(near_own, far_own))
    ring.far(first_panel, slab // 2)
    second_panel = ring.near(up_w[:, FIRST:])
    ring.far(second_panel, slab // 2)
    ring.far(near_panel, FIRST)
    far_panel = ring.near(far_own)
    ring.far(far_panel, FIRST)

    mine, theirs = normed_slabs(place, acts, gains, slab)
    got = send(theirs, zl=1)

    def partial_sums(panel):
        def product(rows):
            near = sum(dot(rows[k], panel[k]) for k in (0, 1, 3))
            return near + dot(rows[2, :, :slab // 2], panel[2][0]) + dot(rows[2, :, slab // 2:], panel[2][1])

        own, other = product(mine), product(got)
        return own + send(other.astype(BF16), zl=1).astype(F32)

    gate, first, second = partial_sums(gate_panel), partial_sums(first_panel), partial_sums(second_panel)
    kept = [(silu(gate[:, :FIRST]) * first).astype(BF16), (silu(gate[:, FIRST:]) * second).astype(BF16)]
    theirs = [send(h, zl=1) for h in kept]
    theirs[1] = after(theirs[1], far_panel[1], far_panel[3])
    hidden = []
    for pair in (kept, theirs):
        hidden += pair + [send(h, core=1) for h in pair]

    products = [down_product(hidden, near_panel, far_panel, chunk) for chunk in CHUNKS]
    pieces = []
    for chunk, (total, sent) in zip(CHUNKS, products):
        came = [send(sent[j - 1], y=j) for j in (1, 3, 2)]
        total = after(total, products[-1][0])
        for value in came:
            total = total + value.astype(F32)
        total = total.astype(BF16)
        sums = [send(total[b * part:(b + 1) * part], layer=1, zh=a, zl=b) for b in range(2) for a in range(2)]
        piece = with_residual(place, acts, sums, chunk)
        own = [piece, send(piece, y=-1), send(piece, y=2), send(piece, y=1)]
        pieces += own + [send(p, core=1) for p in own]
    return assembled(place, pieces, acts.shape[2])


def solution(mesh):
    in_specs = (
        P(None, "fsdp", None),
        P(),
        P("fsdp", "section"),
        P("fsdp", "section"),
        P("section", "fsdp"),
    )
    out_specs = P("section", "fsdp", None)
    return jax.shard_map(local, mesh=mesh, in_specs=in_specs, out_specs=out_specs, check_vma=False)
```

```python
import functools

import jax
import jax.numpy as jnp
from jax import lax
from jax.experimental import pallas as pl
from jax.experimental.pallas import tpu as pltpu
from jax.sharding import PartitionSpec as P

AXES = (("layer", 2), ("zh", 2), ("y", 4), ("core", 2), ("x", 4), ("zl", 2))
FIRST = 512
DEPTH = 3
CHUNKS = ((0, 3), (1, 2))
BF16, F32 = jnp.bfloat16, jnp.float32
ROOM = pltpu.CompilerParams(vmem_limit_bytes=40 << 20)


def decode(index):
    place = {}
    for name, size in reversed(AXES):
        place[name] = index % size
        index //= size
    return place


def encode(place):
    index = 0
    for name, size in AXES:
        index = index * size + place[name] % size
    return index


def send(value, **moves):
    pairs = []
    for index in range(256):
        place = decode(index)
        for name, by in moves.items():
            place[name] += by
        pairs.append((index, encode(place)))
    return lax.ppermute(value, ("section", "fsdp"), pairs)


def after(value, *others):
    return lax.optimization_barrier((value, *others))[0]


def dot(a, b):
    return jnp.dot(a, b, preferred_element_type=F32)


def silu(v):
    return v / (1 + jnp.exp(-v))


def turned(value, way):
    pairs = []
    for index in range(256):
        place = decode(index)
        place["x"] += way * (1 - 2 * place["core"])
        pairs.append((index, encode(place)))
    return lax.ppermute(value, ("section", "fsdp"), pairs)


class Ring:
    def __init__(self):
        self.sent = []

    def turn(self, value, way):
        if len(self.sent) >= DEPTH:
            value = after(value, self.sent[-DEPTH])
        self.sent.append(turned(value, way))
        return self.sent[-1]

    def near(self, shard):
        back = self.turn(shard, 1)
        return [shard, self.turn(shard, -1), None, back]

    def far(self, panel, split):
        panel[2] = (self.turn(panel[3][:split], 1), self.turn(panel[1][split:], -1))


def column(place, core, k, b, size):
    slab = lax.rem(place[3] + k + core * (4 - 2 * k), 4)
    return pl.multiple_of((slab * 2 + lax.rem(place[4] + b, 2)) * size, size)


def norm_kernel(place, acts, gains, mine, theirs, normed):
    size = mine.shape[2]
    widened = acts[0].astype(F32)
    meansq = jnp.mean(widened * widened, axis=-1, keepdims=True)
    normed[...] = (widened * lax.rsqrt(meansq + 1e-05) * gains[pl.ds(place[0], 1), :]).astype(BF16)
    for k in range(4):
        mine[k] = normed[:, pl.ds(column(place, place[2], k, 0, size), size)]
        theirs[k] = normed[:, pl.ds(column(place, place[2], k, 1, size), size)]


def normed_slabs(place, acts, gains, slab):
    tokens, width = acts.shape[1:]
    part = tokens // 4
    shape = jax.ShapeDtypeStruct((4, tokens, slab), BF16)
    spec = pl.BlockSpec((4, part, slab), lambda i, place: (0, i, 0))
    return pl.pallas_call(
        norm_kernel,
        grid_spec=pltpu.PrefetchScalarGridSpec(
            num_scalar_prefetch=1,
            grid=(4,),
            in_specs=[
                pl.BlockSpec((1, part, width), lambda i, place: (place[0], lax.rem(place[1] + i, 4), 0)),
                pl.BlockSpec(gains.shape, lambda i, place: (0, 0)),
            ],
            out_specs=[spec, spec],
            scratch_shapes=[pltpu.VMEM((part, width), BF16)],
        ),
        out_shape=[shape, shape],
        compiler_params=ROOM,
    )(place, acts, gains)


def down_kernel(chunk, *refs):
    hidden, panels, (kept, sent) = refs[:8], list(refs[8:-2]), refs[-2:]
    size = panels[0].shape[1]
    part = kept.shape[0] // 2
    first = hidden[0].shape[1]
    for n, k in enumerate(chunk):
        rows = []
        if k == 2:
            for _ in range(2):
                panel = panels.pop(0)
                rows += [panel[:first], panel[first:]]
        else:
            panel = panels.pop(0)
            count = panel.shape[0] // 2
            rows = [panel[:first], panel[first:count], panel[count:count + first], panel[count + first:]]
        columns = slice(n * size, (n + 1) * size)
        for b in range(2):
            product = sum(dot(hidden[4 * b + i][...], rows[i]) for i in range(4))
            kept[b * part:(b + 1) * part, columns] = product[:part]
            for j in range(3):
                sent[j, b * part:(b + 1) * part, columns] = product[(j + 1) * part:(j + 2) * part].astype(BF16)


def down_product(hidden, down, chunk):
    part, size = hidden[0].shape[0] // 2, down[0].shape[1] * len(chunk)
    vmem = pl.BlockSpec(memory_space=pltpu.VMEM)
    flat = []
    for k in chunk:
        flat += down[k] if k == 2 else [down[k]]
    return pl.pallas_call(
        functools.partial(down_kernel, chunk),
        in_specs=[vmem] * (8 + len(flat)),
        out_specs=[vmem, vmem],
        out_shape=[jax.ShapeDtypeStruct((part, size), F32), jax.ShapeDtypeStruct((3, part, size), BF16)],
        compiler_params=ROOM,
    )(*hidden, *flat)


def residual_kernel(chunk, place, acts, *refs):
    out = refs[-1]
    size = refs[0].shape[1] // len(chunk)
    for b in range(2):
        for i, k in enumerate(chunk):
            columns = slice(i * size, (i + 1) * size)
            first = pl.multiple_of(column(place, place[2], k, b, 2 * size) + place[2] * size, size)
            total = acts[0, :, pl.ds(first, size)].astype(F32) + refs[2 * b][:, columns].astype(F32) + refs[2 * b + 1][:, columns].astype(F32)
            first = (len(chunk) * b + i) * size
            out[:, first:first + size] = total.astype(BF16)


def with_residual(place, acts, sums, chunk):
    part, size = sums[0].shape
    block = pl.BlockSpec((part, size), lambda i, place: (0, 0))
    return pl.pallas_call(
        functools.partial(residual_kernel, chunk),
        grid_spec=pltpu.PrefetchScalarGridSpec(
            num_scalar_prefetch=1,
            grid=(1,),
            in_specs=[pl.BlockSpec((1, part, acts.shape[2]), lambda i, place: (1 - place[0], place[1], 0))] + [block] * 4,
            out_specs=pl.BlockSpec((part, 2 * size), lambda i, place: (0, 0)),
        ),
        out_shape=jax.ShapeDtypeStruct((part, 2 * size), BF16),
        compiler_params=ROOM,
    )(place, acts, *sums)


def assembly_kernel(place, *refs):
    out = refs[-1]
    for j in range(4):

        @pl.when(pl.program_id(0) == j)
        def _():
            for c, chunk in enumerate(CHUNKS):
                for i in range(2):
                    piece = refs[8 * c + 4 * i + j]
                    size = piece.shape[1] // (2 * len(chunk))
                    core = lax.rem(place[2] + i, 2)
                    for b in range(2):
                        for n, k in enumerate(chunk):
                            first = pl.multiple_of(column(place, core, k, b, 2 * size) + core * size, size)
                            start = (len(chunk) * b + n) * size
                            out[0, :, pl.ds(first, size)] = piece[:, start:start + size]


def assembled(place, pieces, width):
    part = pieces[0].shape[0]
    return pl.pallas_call(
        assembly_kernel,
        grid_spec=pltpu.PrefetchScalarGridSpec(
            num_scalar_prefetch=1,
            grid=(4,),
            in_specs=[pl.BlockSpec(p.shape, lambda i, place: (0, 0)) for p in pieces],
            out_specs=pl.BlockSpec((1, part, width), lambda i, place: (0, lax.rem(place[1] + i, 4), 0)),
        ),
        out_shape=jax.ShapeDtypeStruct((1, 4 * part, width), BF16),
        compiler_params=ROOM,
    )(place, *pieces)


def local(acts, gains, gate_w, up_w, down_w):
    section, fsdp = lax.axis_index("section"), lax.axis_index("fsdp")
    core = section % 2
    place = jnp.stack([section // 16, section // 2 % 4, core, fsdp // 2, fsdp % 2]).astype(jnp.int32)
    tokens = acts.shape[1]
    slab = gate_w.shape[0]
    part = tokens // 4

    low, high = down_w[:, :slab // 2], down_w[:, slab // 2:]
    down_own = jnp.concatenate([jnp.where(core == 0, low, high), send(jnp.where(core == 0, high, low), core=1)], 0)
    ring = Ring()
    gate_panel = ring.near(gate_w)
    first_panel = ring.near(up_w[:, :FIRST])
    ring.far(gate_panel, slab // 2)
    second_panel = ring.near(after(up_w[:, FIRST:], down_own))
    ring.far(first_panel, slab // 2)
    ring.far(second_panel, slab // 2)
    down_panel = ring.near(down_own)
    ring.far(down_panel, down_w.shape[0])

    mine, theirs = normed_slabs(place, acts, gains, slab)
    got = send(theirs, zl=1)

    def partial_sums(panel):
        def product(rows):
            near = sum(dot(rows[k], panel[k]) for k in (0, 1, 3))
            return near + dot(rows[2, :, :slab // 2], panel[2][0]) + dot(rows[2, :, slab // 2:], panel[2][1])

        own, other = product(mine), product(got)
        return own + send(other.astype(BF16), zl=1).astype(F32)

    gate, first, second = partial_sums(gate_panel), partial_sums(first_panel), partial_sums(second_panel)
    kept = [(silu(gate[:, :FIRST]) * first).astype(BF16), (silu(gate[:, FIRST:]) * second).astype(BF16)]
    theirs = [send(h, zl=1) for h in kept]
    theirs[1] = after(theirs[1], down_panel[1], down_panel[3])
    hidden = []
    for pair in (kept, theirs):
        hidden += pair + [send(h, core=1) for h in pair]

    products = [down_product(hidden, down_panel, chunk) for chunk in CHUNKS]
    pieces = []
    for chunk, (total, sent) in zip(CHUNKS, products):
        came = [send(sent[j - 1], y=j) for j in (1, 3, 2)]
        total = after(total, products[-1][0])
        for value in came:
            total = total + value.astype(F32)
        total = total.astype(BF16)
        sums = [send(total[b * part:(b + 1) * part], layer=1, zh=a, zl=b) for b in range(2) for a in range(2)]
        piece = with_residual(place, acts, sums, chunk)
        own = [piece, send(piece, y=-1), send(piece, y=2), send(piece, y=1)]
        pieces += own + [send(p, core=1) for p in own]
    return assembled(place, pieces, acts.shape[2])


def solution(mesh):
    in_specs = (
        P(None, "fsdp", None),
        P(),
        P("fsdp", "section"),
        P("fsdp", "section"),
        P("section", "fsdp"),
    )
    out_specs = P("section", "fsdp", None)
    return jax.shard_map(local, mesh=mesh, in_specs=in_specs, out_specs=out_specs, check_vma=False)
```

```python
import functools

import jax
import jax.numpy as jnp
from jax import lax
from jax.experimental import pallas as pl
from jax.experimental.pallas import tpu as pltpu
from jax.sharding import PartitionSpec as P

AXES = (("layer", 2), ("zh", 2), ("y", 4), ("core", 2), ("x", 4), ("zl", 2))
FIRST = 512
DEPTH = 3
CHUNKS = ((0, 3), (1, 2))
BF16, F32 = jnp.bfloat16, jnp.float32
ROOM = pltpu.CompilerParams(vmem_limit_bytes=40 << 20)


def decode(index):
    place = {}
    for name, size in reversed(AXES):
        place[name] = index % size
        index //= size
    return place


def encode(place):
    index = 0
    for name, size in AXES:
        index = index * size + place[name] % size
    return index


def send(value, **moves):
    pairs = []
    for index in range(256):
        place = decode(index)
        for name, by in moves.items():
            place[name] += by
        pairs.append((index, encode(place)))
    return lax.ppermute(value, ("section", "fsdp"), pairs)


def after(value, *others):
    return lax.optimization_barrier((value, *others))[0]


def dot(a, b):
    return jnp.dot(a, b, preferred_element_type=F32)


def silu(v):
    return v / (1 + jnp.exp(-v))


def turned(value, way):
    pairs = []
    for index in range(256):
        place = decode(index)
        place["x"] += way * (1 - 2 * place["core"])
        pairs.append((index, encode(place)))
    return lax.ppermute(value, ("section", "fsdp"), pairs)


class Ring:
    def __init__(self):
        self.sent = []

    def turn(self, value, way):
        if len(self.sent) >= DEPTH:
            value = after(value, self.sent[-DEPTH])
        self.sent.append(turned(value, way))
        return self.sent[-1]

    def near(self, shard):
        back = self.turn(shard, 1)
        return [shard, self.turn(shard, -1), None, back]

    def far(self, panel, split):
        panel[2] = (self.turn(panel[3][:split], 1), self.turn(panel[1][split:], -1))


def column(place, core, k, b, size):
    slab = lax.rem(place[3] + k + core * (4 - 2 * k), 4)
    return pl.multiple_of((slab * 2 + lax.rem(place[4] + b, 2)) * size, size)


def norm_kernel(place, acts, gains, mine, theirs, normed):
    size = mine.shape[2]
    widened = acts[0].astype(F32)
    meansq = jnp.mean(widened * widened, axis=-1, keepdims=True)
    normed[...] = (widened * lax.rsqrt(meansq + 1e-05) * gains[pl.ds(place[0], 1), :]).astype(BF16)
    for k in range(4):
        mine[k] = normed[:, pl.ds(column(place, place[2], k, 0, size), size)]
        theirs[k] = normed[:, pl.ds(column(place, place[2], k, 1, size), size)]


def normed_slabs(place, acts, gains, slab):
    tokens, width = acts.shape[1:]
    part = tokens // 4
    shape = jax.ShapeDtypeStruct((4, tokens, slab), BF16)
    spec = pl.BlockSpec((4, part, slab), lambda i, place: (0, i, 0))
    return pl.pallas_call(
        norm_kernel,
        grid_spec=pltpu.PrefetchScalarGridSpec(
            num_scalar_prefetch=1,
            grid=(4,),
            in_specs=[
                pl.BlockSpec((1, part, width), lambda i, place: (place[0], lax.rem(place[1] + i, 4), 0)),
                pl.BlockSpec(gains.shape, lambda i, place: (0, 0)),
            ],
            out_specs=[spec, spec],
            scratch_shapes=[pltpu.VMEM((part, width), BF16)],
        ),
        out_shape=[shape, shape],
        compiler_params=ROOM,
    )(place, acts, gains)


def down_kernel(chunk, *refs):
    hidden, panels, (kept, sent) = refs[:8], list(refs[8:-2]), refs[-2:]
    size = panels[0].shape[1]
    part = kept.shape[0] // 2
    first = hidden[0].shape[1]
    for n, k in enumerate(chunk):
        rows = []
        if k == 2:
            for _ in range(2):
                panel = panels.pop(0)
                rows += [panel[:first], panel[first:]]
        else:
            panel = panels.pop(0)
            count = panel.shape[0] // 2
            rows = [panel[:first], panel[first:count], panel[count:count + first], panel[count + first:]]
        columns = slice(n * size, (n + 1) * size)
        for b in range(2):
            product = sum(dot(hidden[4 * b + i][...], rows[i]) for i in range(4))
            kept[b * part:(b + 1) * part, columns] = product[:part]
            for j in range(3):
                sent[j, b * part:(b + 1) * part, columns] = product[(j + 1) * part:(j + 2) * part].astype(BF16)


def down_product(hidden, down, chunk):
    part, size = hidden[0].shape[0] // 2, down[0].shape[1] * len(chunk)
    vmem = pl.BlockSpec(memory_space=pltpu.VMEM)
    flat = []
    for k in chunk:
        flat += down[k] if k == 2 else [down[k]]
    return pl.pallas_call(
        functools.partial(down_kernel, chunk),
        in_specs=[vmem] * (8 + len(flat)),
        out_specs=[vmem, vmem],
        out_shape=[jax.ShapeDtypeStruct((part, size), F32), jax.ShapeDtypeStruct((3, part, size), BF16)],
        compiler_params=ROOM,
    )(*hidden, *flat)


def residual_kernel(chunk, place, acts, *refs):
    out = refs[-1]
    size = refs[0].shape[1] // len(chunk)
    for b in range(2):
        for i, k in enumerate(chunk):
            columns = slice(i * size, (i + 1) * size)
            first = pl.multiple_of(column(place, place[2], k, b, 2 * size) + place[2] * size, size)
            total = acts[0, :, pl.ds(first, size)].astype(F32) + refs[2 * b][:, columns].astype(F32) + refs[2 * b + 1][:, columns].astype(F32)
            first = (len(chunk) * b + i) * size
            out[:, first:first + size] = total.astype(BF16)


def with_residual(place, acts, sums, chunk):
    part, size = sums[0].shape
    block = pl.BlockSpec((part, size), lambda i, place: (0, 0))
    return pl.pallas_call(
        functools.partial(residual_kernel, chunk),
        grid_spec=pltpu.PrefetchScalarGridSpec(
            num_scalar_prefetch=1,
            grid=(1,),
            in_specs=[pl.BlockSpec((1, part, acts.shape[2]), lambda i, place: (1 - place[0], place[1], 0))] + [block] * 4,
            out_specs=pl.BlockSpec((part, 2 * size), lambda i, place: (0, 0)),
        ),
        out_shape=jax.ShapeDtypeStruct((part, 2 * size), BF16),
        compiler_params=ROOM,
    )(place, acts, *sums)


def assembly_kernel(place, *refs):
    out = refs[-1]
    for j in range(4):

        @pl.when(pl.program_id(0) == j)
        def _():
            for c, chunk in enumerate(CHUNKS):
                for i in range(2):
                    piece = refs[8 * c + 4 * i + j]
                    size = piece.shape[1] // (2 * len(chunk))
                    core = lax.rem(place[2] + i, 2)
                    for b in range(2):
                        for n, k in enumerate(chunk):
                            first = pl.multiple_of(column(place, core, k, b, 2 * size) + core * size, size)
                            start = (len(chunk) * b + n) * size
                            out[0, :, pl.ds(first, size)] = piece[:, start:start + size]


def assembled(place, pieces, width):
    part = pieces[0].shape[0]
    return pl.pallas_call(
        assembly_kernel,
        grid_spec=pltpu.PrefetchScalarGridSpec(
            num_scalar_prefetch=1,
            grid=(4,),
            in_specs=[pl.BlockSpec(p.shape, lambda i, place: (0, 0)) for p in pieces],
            out_specs=pl.BlockSpec((1, part, width), lambda i, place: (0, lax.rem(place[1] + i, 4), 0)),
        ),
        out_shape=jax.ShapeDtypeStruct((1, 4 * part, width), BF16),
        compiler_params=ROOM,
    )(place, *pieces)


def local(acts, gains, gate_w, up_w, down_w):
    section, fsdp = lax.axis_index("section"), lax.axis_index("fsdp")
    core = section % 2
    place = jnp.stack([section // 16, section // 2 % 4, core, fsdp // 2, fsdp % 2]).astype(jnp.int32)
    tokens = acts.shape[1]
    slab = gate_w.shape[0]
    part = tokens // 4

    low, high = down_w[:, :slab // 2], down_w[:, slab // 2:]
    down_own = jnp.concatenate([jnp.where(core == 0, low, high), send(jnp.where(core == 0, high, low), core=1)], 0)
    ring = Ring()
    gate_panel = ring.near(gate_w)
    first_panel = ring.near(up_w[:, :FIRST])
    ring.far(gate_panel, slab // 2)
    second_panel = ring.near(after(up_w[:, FIRST:], down_own))
    ring.far(first_panel, slab // 2)
    ring.far(second_panel, slab // 2)
    down_panel = ring.near(down_own)
    ring.far(down_panel, down_w.shape[0])

    mine, theirs = normed_slabs(place, acts, gains, slab)
    got = send(theirs, zl=1)

    def partial_sums(panel):
        def product(rows):
            near = sum(dot(rows[k], panel[k]) for k in (0, 1, 3))
            return near + dot(rows[2, :, :slab // 2], panel[2][0]) + dot(rows[2, :, slab // 2:], panel[2][1])

        own, other = product(mine), product(got)
        return own + send(other.astype(BF16), zl=1).astype(F32)

    gate, first, second = partial_sums(gate_panel), partial_sums(first_panel), partial_sums(second_panel)
    kept = [(silu(gate[:, :FIRST]) * first).astype(BF16), (silu(gate[:, FIRST:]) * second).astype(BF16)]
    theirs = [send(h, zl=1) for h in kept]
    theirs[1] = after(theirs[1], down_panel[1], down_panel[3])
    hidden = []
    for pair in (kept, theirs):
        hidden += pair + [send(h, core=1) for h in pair]

    products = [down_product(hidden, down_panel, chunk) for chunk in CHUNKS]
    came = [[send(sent[j - 1], y=j) for j in (1, 3, 2)] for _, sent in products]
    pieces, totals = [], []
    for (total, _), values in zip(products, came):
        total = after(total, products[-1][0])
        for value in values:
            total = total + value.astype(F32)
        totals.append(total.astype(BF16))
    sums = []
    for total in totals:
        low, high = total[:part], total[part:]
        if not sums:
            high = after(high, *came[-1])
        sums.append([send(half, layer=1, zh=a, zl=b) for b, half in enumerate((low, high)) for a in range(2)])
    for chunk, values in zip(CHUNKS, sums):
        piece = with_residual(place, acts, values, chunk)
        late = last = piece
        if values is sums[0]:
            late, last = after(piece, *sums[-1][:2]), after(piece, *sums[-1])
        own = [last, send(piece, y=-1), send(late, y=2), send(last, y=1)]
        pieces += own + [send(p, core=1) for p in own]
    return assembled(place, pieces, acts.shape[2])


def solution(mesh):
    in_specs = (
        P(None, "fsdp", None),
        P(),
        P("fsdp", "section"),
        P("fsdp", "section"),
        P("section", "fsdp"),
    )
    out_specs = P("section", "fsdp", None)
    return jax.shard_map(local, mesh=mesh, in_specs=in_specs, out_specs=out_specs, check_vma=False)
```

```python
import functools

import jax
import jax.numpy as jnp
from jax import lax
from jax.experimental import pallas as pl
from jax.experimental.pallas import tpu as pltpu
from jax.sharding import PartitionSpec as P

AXES = (("layer", 2), ("zh", 2), ("y", 4), ("core", 2), ("x", 4), ("zl", 2))
FIRST = 512
CHUNKS = ((0, 3), (1, 2))
BF16, F32 = jnp.bfloat16, jnp.float32
ROOM = pltpu.CompilerParams(vmem_limit_bytes=40 << 20)


def decode(index):
    place = {}
    for name, size in reversed(AXES):
        place[name] = index % size
        index //= size
    return place


def encode(place):
    index = 0
    for name, size in AXES:
        index = index * size + place[name] % size
    return index


def send(value, **moves):
    pairs = []
    for index in range(256):
        place = decode(index)
        for name, by in moves.items():
            place[name] += by
        pairs.append((index, encode(place)))
    return lax.ppermute(value, ("section", "fsdp"), pairs)


def after(value, *others):
    return lax.optimization_barrier((value, *others))[0]


def dot(a, b):
    return jnp.dot(a, b, preferred_element_type=F32)


def silu(v):
    return v / (1 + jnp.exp(-v))


def turned(value, way):
    pairs = []
    for index in range(256):
        place = decode(index)
        place["x"] += way * (1 - 2 * place["core"])
        pairs.append((index, encode(place)))
    return lax.ppermute(value, ("section", "fsdp"), pairs)


def crossed(value, a):
    pairs = []
    for index in range(256):
        place = decode(index)
        place["zl"] += place["zh"]
        place["zh"] += a
        place["layer"] += 1
        pairs.append((index, encode(place)))
    return lax.ppermute(value, ("section", "fsdp"), pairs)


class Ring:
    def __init__(self, depth):
        self.sent, self.depth = [], depth

    def turn(self, value, way):
        if len(self.sent) >= self.depth:
            value = after(value, self.sent[-self.depth])
        self.sent.append(turned(value, way))
        return self.sent[-1]

    def near(self, shard):
        back = self.turn(shard, 1)
        return [shard, self.turn(shard, -1), None, back]

    def far(self, panel, split):
        panel[2] = (self.turn(panel[3][:split], 1), self.turn(panel[1][split:], -1))


def column(place, core, k, b, size):
    slab = lax.rem(place[3] + k + core * (4 - 2 * k), 4)
    return pl.multiple_of((slab * 2 + lax.rem(place[4] + b, 2)) * size, size)


def norm_kernel(place, acts, gains, mine, theirs, normed):
    size = mine.shape[2]
    widened = acts[0].astype(F32)
    meansq = jnp.mean(widened * widened, axis=-1, keepdims=True)
    normed[...] = (widened * lax.rsqrt(meansq + 1e-05) * gains[pl.ds(place[0], 1), :]).astype(BF16)
    for k in range(4):
        mine[k] = normed[:, pl.ds(column(place, place[2], k, 0, size), size)]
        theirs[k] = normed[:, pl.ds(column(place, place[2], k, 1, size), size)]


def normed_slabs(place, acts, gains, slab):
    tokens, width = acts.shape[1:]
    part = tokens // 4
    shape = jax.ShapeDtypeStruct((4, tokens, slab), BF16)
    spec = pl.BlockSpec((4, part, slab), lambda i, place: (0, i, 0))
    return pl.pallas_call(
        norm_kernel,
        grid_spec=pltpu.PrefetchScalarGridSpec(
            num_scalar_prefetch=1,
            grid=(4,),
            in_specs=[
                pl.BlockSpec((1, part, width), lambda i, place: (place[0], lax.rem(place[1] + i, 4), 0)),
                pl.BlockSpec(gains.shape, lambda i, place: (0, 0)),
            ],
            out_specs=[spec, spec],
            scratch_shapes=[pltpu.VMEM((part, width), BF16)],
        ),
        out_shape=[shape, shape],
        compiler_params=ROOM,
    )(place, acts, gains)


def down_kernel(chunk, *refs):
    hidden, panels, (kept, sent) = refs[:8], list(refs[8:-2]), refs[-2:]
    size = panels[0].shape[1]
    part = kept.shape[0] // 2
    first = hidden[0].shape[1]
    for n, k in enumerate(chunk):
        rows = []
        if k == 2:
            for _ in range(2):
                panel = panels.pop(0)
                rows += [panel[:first], panel[first:]]
        else:
            panel = panels.pop(0)
            count = panel.shape[0] // 2
            rows = [panel[:first], panel[first:count], panel[count:count + first], panel[count + first:]]
        columns = slice(n * size, (n + 1) * size)
        for b in range(2):
            product = sum(dot(hidden[4 * b + i][...], rows[i]) for i in range(4))
            kept[b * part:(b + 1) * part, columns] = product[:part]
            for j in range(3):
                sent[j, b * part:(b + 1) * part, columns] = product[(j + 1) * part:(j + 2) * part].astype(BF16)


def down_product(hidden, down, chunk):
    part, size = hidden[0].shape[0] // 2, down[0].shape[1] * len(chunk)
    vmem = pl.BlockSpec(memory_space=pltpu.VMEM)
    flat = []
    for k in chunk:
        flat += down[k] if k == 2 else [down[k]]
    return pl.pallas_call(
        functools.partial(down_kernel, chunk),
        in_specs=[vmem] * (8 + len(flat)),
        out_specs=[vmem, vmem],
        out_shape=[jax.ShapeDtypeStruct((part, size), F32), jax.ShapeDtypeStruct((3, part, size), BF16)],
        compiler_params=ROOM,
    )(*hidden, *flat)


def residual_kernel(chunk, place, acts, *refs):
    refs, out = refs[:-1], refs[-1]
    size = refs[0].shape[1] // len(chunk)
    each = len(refs) // 2
    for b in range(2):
        turn = b if each == 2 else place[5] + b
        for i, k in enumerate(chunk):
            columns = slice(i * size, (i + 1) * size)
            first = pl.multiple_of(column(place, place[2], k, turn, 2 * size) + place[2] * size, size)
            total = acts[0, :, pl.ds(first, size)].astype(F32)
            for value in refs[each * b:each * (b + 1)]:
                total += value[:, columns].astype(F32)
            first = (len(chunk) * b + i) * size
            out[:, first:first + size] = total.astype(BF16)


def with_residual(place, acts, sums, chunk):
    part, size = sums[0].shape
    block = pl.BlockSpec((part, size), lambda i, place: (0, 0))
    return pl.pallas_call(
        functools.partial(residual_kernel, chunk),
        grid_spec=pltpu.PrefetchScalarGridSpec(
            num_scalar_prefetch=1,
            grid=(1,),
            in_specs=[pl.BlockSpec((1, part, acts.shape[2]), lambda i, place: (1 - place[0], place[1], 0))] + [block] * len(sums),
            out_specs=pl.BlockSpec((part, 2 * size), lambda i, place: (0, 0)),
        ),
        out_shape=jax.ShapeDtypeStruct((part, 2 * size), BF16),
        compiler_params=ROOM,
    )(place, acts, *sums)


def assembly_kernel(place, *refs):
    out = refs[-1]
    for j in range(4):

        @pl.when(pl.program_id(0) == j)
        def _():
            for c, chunk in enumerate(CHUNKS):
                for i in range(2):
                    piece = refs[8 * c + 4 * i + j]
                    size = piece.shape[1] // (2 * len(chunk))
                    core = lax.rem(place[2] + i, 2)
                    for b in range(2):
                        for n, k in enumerate(chunk):
                            first = pl.multiple_of(column(place, core, k, b + c * place[5], 2 * size) + core * size, size)
                            start = (len(chunk) * b + n) * size
                            out[0, :, pl.ds(first, size)] = piece[:, start:start + size]


def assembled(place, pieces, width):
    part = pieces[0].shape[0]
    return pl.pallas_call(
        assembly_kernel,
        grid_spec=pltpu.PrefetchScalarGridSpec(
            num_scalar_prefetch=1,
            grid=(4,),
            in_specs=[pl.BlockSpec(p.shape, lambda i, place: (0, 0)) for p in pieces],
            out_specs=pl.BlockSpec((1, part, width), lambda i, place: (0, lax.rem(place[1] + i, 4), 0)),
        ),
        out_shape=jax.ShapeDtypeStruct((1, 4 * part, width), BF16),
        compiler_params=ROOM,
    )(place, *pieces)


def local(acts, gains, gate_w, up_w, down_w):
    section, fsdp = lax.axis_index("section"), lax.axis_index("fsdp")
    core, zh = section % 2, section // 8 % 2
    place = jnp.stack([section // 16, section // 2 % 4, core, fsdp // 2, fsdp % 2, zh]).astype(jnp.int32)
    tokens = acts.shape[1]
    slab = gate_w.shape[0]
    part = tokens // 4

    low, high = down_w[:, :slab // 2], down_w[:, slab // 2:]
    down_own = jnp.concatenate([jnp.where(core == 0, low, high), send(jnp.where(core == 0, high, low), core=1)], 0)
    ring = Ring(3)
    gate_panel = ring.near(gate_w)
    first_panel = ring.near(up_w[:, :FIRST])
    ring.far(gate_panel, slab // 2)
    second_panel = ring.near(after(up_w[:, FIRST:], down_own))
    ring.far(first_panel, slab // 2)
    ring.far(second_panel, slab // 2)
    ring.depth = 3
    down_panel = ring.near(down_own)

    mine, theirs = normed_slabs(place, acts, gains, slab)
    got = send(theirs, zl=1)

    def partial_sums(panel):
        def product(rows):
            near = sum(dot(rows[k], panel[k]) for k in (0, 1, 3))
            return near + dot(rows[2, :, :slab // 2], panel[2][0]) + dot(rows[2, :, slab // 2:], panel[2][1])

        own, other = product(mine), product(got)
        return own + send(other.astype(BF16), zl=1).astype(F32)

    gate, first, second = partial_sums(gate_panel), partial_sums(first_panel), partial_sums(second_panel)
    kept = [(silu(gate[:, :FIRST]) * first).astype(BF16), (silu(gate[:, FIRST:]) * second).astype(BF16)]
    theirs = [send(h, zl=1) for h in kept]
    near = [send(h, core=1) for h in kept]
    theirs[1] = after(theirs[1], *near)
    hidden = kept + near + theirs + [send(h, core=1) for h in theirs]
    down_panel[1], down_panel[3] = after(down_panel[1], hidden[7]), after(down_panel[3], hidden[7])
    ring.far(down_panel, down_w.shape[0])

    products = [down_product(hidden, down_panel, chunk) for chunk in CHUNKS]
    came = [[send(sent[j - 1], y=j) for j in (1, 3, 2)] for _, sent in products]
    pieces, totals = [], []
    for (total, _), values in zip(products, came):
        total = after(total, products[-1][0])
        for value in values:
            total = total + value.astype(F32)
        totals.append(total)

    low, high = totals[0][:part].astype(BF16), totals[0][part:].astype(BF16)
    sums = [[send(half, layer=1, zh=a, zl=b) for b, half in enumerate((low, after(high, *came[-1]))) for a in range(2)]]
    low, high = totals[1][:part], totals[1][part:]
    away = after(jnp.where(zh == 0, high, low).astype(BF16), *sums[0][:2])
    total = (jnp.where(zh == 0, low, high) + send(away, zh=1).astype(F32)).astype(BF16)
    sums.append([crossed(total, a) for a in range(2)])
    for chunk, values in zip(CHUNKS, sums):
        piece = with_residual(place, acts, values, chunk)
        late = last = piece
        if values is sums[0]:
            late, last = after(piece, *sums[-1][:2]), after(piece, *sums[-1])
        own = [last, send(piece, y=-1), send(late, y=2), send(last, y=1)]
        pieces += own + [send(p, core=1) for p in own]
    return assembled(place, pieces, acts.shape[2])


def solution(mesh):
    in_specs = (
        P(None, "fsdp", None),
        P(),
        P("fsdp", "section"),
        P("fsdp", "section"),
        P("section", "fsdp"),
    )
    out_specs = P("section", "fsdp", None)
    return jax.shard_map(local, mesh=mesh, in_specs=in_specs, out_specs=out_specs, check_vma=False)
```

```python
import functools

import jax
import jax.numpy as jnp
from jax import lax
from jax.experimental import pallas as pl
from jax.experimental.pallas import tpu as pltpu
from jax.sharding import PartitionSpec as P

AXES = (("layer", 2), ("zh", 2), ("y", 4), ("core", 2), ("x", 4), ("zl", 2))
FIRST = 512
CHUNKS = ((0, 3), (1, 2))
BF16, F32 = jnp.bfloat16, jnp.float32
ROOM = pltpu.CompilerParams(vmem_limit_bytes=40 << 20)


def decode(index):
    place = {}
    for name, size in reversed(AXES):
        place[name] = index % size
        index //= size
    return place


def encode(place):
    index = 0
    for name, size in AXES:
        index = index * size + place[name] % size
    return index


def send(value, **moves):
    pairs = []
    for index in range(256):
        place = decode(index)
        for name, by in moves.items():
            place[name] += by
        pairs.append((index, encode(place)))
    return lax.ppermute(value, ("section", "fsdp"), pairs)


def after(value, *others):
    return lax.optimization_barrier((value, *others))[0]


def dot(a, b):
    return jnp.dot(a, b, preferred_element_type=F32)


def silu(v):
    return v / (1 + jnp.exp(-v))


def turned(value, way):
    pairs = []
    for index in range(256):
        place = decode(index)
        place["x"] += way * (1 - 2 * place["core"])
        pairs.append((index, encode(place)))
    return lax.ppermute(value, ("section", "fsdp"), pairs)


class Ring:
    def __init__(self, depth):
        self.sent, self.depth = [], depth

    def turn(self, value, way):
        if len(self.sent) >= self.depth:
            value = after(value, self.sent[-self.depth])
        self.sent.append(turned(value, way))
        return self.sent[-1]

    def near(self, shard):
        back = self.turn(shard, 1)
        return [shard, self.turn(shard, -1), None, back]

    def far(self, panel, split):
        panel[2] = (self.turn(panel[3][:split], 1), self.turn(panel[1][split:], -1))


def column(place, core, k, b, size):
    slab = lax.rem(place[3] + k + core * (4 - 2 * k), 4)
    return pl.multiple_of((slab * 2 + lax.rem(place[4] + b, 2)) * size, size)


def norm_kernel(place, acts, gains, mine, theirs, normed):
    size = mine.shape[2]
    widened = acts[0].astype(F32)
    meansq = jnp.mean(widened * widened, axis=-1, keepdims=True)
    normed[...] = (widened * lax.rsqrt(meansq + 1e-05) * gains[pl.ds(place[0], 1), :]).astype(BF16)
    for k in range(4):
        mine[k] = normed[:, pl.ds(column(place, place[2], k, 0, size), size)]
        theirs[k] = normed[:, pl.ds(column(place, place[2], k, 1, size), size)]


def normed_slabs(place, acts, gains, slab):
    tokens, width = acts.shape[1:]
    part = tokens // 4
    shape = jax.ShapeDtypeStruct((4, tokens, slab), BF16)
    spec = pl.BlockSpec((4, part, slab), lambda i, place: (0, i, 0))
    return pl.pallas_call(
        norm_kernel,
        grid_spec=pltpu.PrefetchScalarGridSpec(
            num_scalar_prefetch=1,
            grid=(4,),
            in_specs=[
                pl.BlockSpec((1, part, width), lambda i, place: (place[0], lax.rem(place[1] + i, 4), 0)),
                pl.BlockSpec(gains.shape, lambda i, place: (0, 0)),
            ],
            out_specs=[spec, spec],
            scratch_shapes=[pltpu.VMEM((part, width), BF16)],
        ),
        out_shape=[shape, shape],
        compiler_params=ROOM,
    )(place, acts, gains)


def down_kernel(chunk, *refs):
    hidden, panels, (kept, sent) = refs[:8], list(refs[8:-2]), refs[-2:]
    size = panels[0].shape[1]
    part = kept.shape[0] // 2
    first = hidden[0].shape[1]
    for n, k in enumerate(chunk):
        rows = []
        if k == 2:
            for _ in range(2):
                panel = panels.pop(0)
                rows += [panel[:first], panel[first:]]
        else:
            panel = panels.pop(0)
            count = panel.shape[0] // 2
            rows = [panel[:first], panel[first:count], panel[count:count + first], panel[count + first:]]
        columns = slice(n * size, (n + 1) * size)
        for b in range(2):
            product = sum(dot(hidden[4 * b + i][...], rows[i]) for i in range(4))
            kept[b * part:(b + 1) * part, columns] = product[:part]
            for j in range(3):
                sent[j, b * part:(b + 1) * part, columns] = product[(j + 1) * part:(j + 2) * part].astype(BF16)


def down_product(hidden, down, chunk):
    part, size = hidden[0].shape[0] // 2, down[0].shape[1] * len(chunk)
    vmem = pl.BlockSpec(memory_space=pltpu.VMEM)
    flat = []
    for k in chunk:
        flat += down[k] if k == 2 else [down[k]]
    return pl.pallas_call(
        functools.partial(down_kernel, chunk),
        in_specs=[vmem] * (8 + len(flat)),
        out_specs=[vmem, vmem],
        out_shape=[jax.ShapeDtypeStruct((part, size), F32), jax.ShapeDtypeStruct((3, part, size), BF16)],
        compiler_params=ROOM,
    )(*hidden, *flat)


def residual_kernel(chunk, place, acts, *refs):
    out = refs[-1]
    size = refs[0].shape[1] // len(chunk)
    for b in range(2):
        for i, k in enumerate(chunk):
            columns = slice(i * size, (i + 1) * size)
            first = pl.multiple_of(column(place, place[2], k, b, 2 * size) + place[2] * size, size)
            total = acts[0, :, pl.ds(first, size)].astype(F32) + refs[2 * b][:, columns].astype(F32) + refs[2 * b + 1][:, columns].astype(F32)
            first = (len(chunk) * b + i) * size
            out[:, first:first + size] = total.astype(BF16)


def with_residual(place, acts, sums, chunk):
    part, size = sums[0].shape
    block = pl.BlockSpec((part, size), lambda i, place: (0, 0))
    return pl.pallas_call(
        functools.partial(residual_kernel, chunk),
        grid_spec=pltpu.PrefetchScalarGridSpec(
            num_scalar_prefetch=1,
            grid=(1,),
            in_specs=[pl.BlockSpec((1, part, acts.shape[2]), lambda i, place: (1 - place[0], place[1], 0))] + [block] * 4,
            out_specs=pl.BlockSpec((part, 2 * size), lambda i, place: (0, 0)),
        ),
        out_shape=jax.ShapeDtypeStruct((part, 2 * size), BF16),
        compiler_params=ROOM,
    )(place, acts, *sums)


def assembly_kernel(place, *refs):
    out = refs[-1]
    for j in range(4):

        @pl.when(pl.program_id(0) == j)
        def _():
            for c, chunk in enumerate(CHUNKS):
                for i in range(2):
                    piece = refs[8 * c + 4 * i + j]
                    size = piece.shape[1] // (2 * len(chunk))
                    core = lax.rem(place[2] + i, 2)
                    for b in range(2):
                        for n, k in enumerate(chunk):
                            first = pl.multiple_of(column(place, core, k, b, 2 * size) + core * size, size)
                            start = (len(chunk) * b + n) * size
                            out[0, :, pl.ds(first, size)] = piece[:, start:start + size]


def assembled(place, pieces, width):
    part = pieces[0].shape[0]
    return pl.pallas_call(
        assembly_kernel,
        grid_spec=pltpu.PrefetchScalarGridSpec(
            num_scalar_prefetch=1,
            grid=(4,),
            in_specs=[pl.BlockSpec(p.shape, lambda i, place: (0, 0)) for p in pieces],
            out_specs=pl.BlockSpec((1, part, width), lambda i, place: (0, lax.rem(place[1] + i, 4), 0)),
        ),
        out_shape=jax.ShapeDtypeStruct((1, 4 * part, width), BF16),
        compiler_params=ROOM,
    )(place, *pieces)


def local(acts, gains, gate_w, up_w, down_w):
    section, fsdp = lax.axis_index("section"), lax.axis_index("fsdp")
    core = section % 2
    place = jnp.stack([section // 16, section // 2 % 4, core, fsdp // 2, fsdp % 2]).astype(jnp.int32)
    tokens = acts.shape[1]
    slab = gate_w.shape[0]
    part = tokens // 4

    low, high = down_w[:, :slab // 2], down_w[:, slab // 2:]
    down_own = jnp.concatenate([jnp.where(core == 0, low, high), send(jnp.where(core == 0, high, low), core=1)], 0)
    ring = Ring(4)
    gate_panel = ring.near(gate_w)
    first_panel = ring.near(up_w[:, :FIRST])
    ring.far(gate_panel, slab // 2)
    second_panel = ring.near(after(up_w[:, FIRST:], down_own))
    ring.far(first_panel, slab // 2)
    second_panel[1], second_panel[3] = after(second_panel[1], *gate_panel[2]), after(second_panel[3], *gate_panel[2])
    ring.far(second_panel, slab // 2)
    ring.depth = 3
    down_panel = ring.near(after(down_own, *first_panel[2]))
    ring.far(down_panel, down_w.shape[0])

    mine, theirs = normed_slabs(place, acts, gains, slab)
    got = send(theirs, zl=1)

    def partial_sums(panel):
        def product(rows):
            near = sum(dot(rows[k], panel[k]) for k in (0, 1, 3))
            return near + dot(rows[2, :, :slab // 2], panel[2][0]) + dot(rows[2, :, slab // 2:], panel[2][1])

        own, other = product(mine), product(got)
        return own + send(other.astype(BF16), zl=1).astype(F32)

    gate, first, second = partial_sums(gate_panel), partial_sums(first_panel), partial_sums(second_panel)
    kept = [(silu(gate[:, :FIRST]) * first).astype(BF16), (silu(gate[:, FIRST:]) * second).astype(BF16)]
    theirs = [send(h, zl=1) for h in kept]
    theirs[1] = after(theirs[1], down_panel[1], down_panel[3])
    hidden = []
    for pair in (kept, theirs):
        hidden += pair + [send(h, core=1) for h in pair]

    products = [down_product(hidden, down_panel, chunk) for chunk in CHUNKS]
    came = [[send(sent[j - 1], y=j) for j in (1, 3, 2)] for _, sent in products]
    pieces, totals = [], []
    for (total, _), values in zip(products, came):
        total = after(total, products[-1][0])
        for value in values:
            total = total + value.astype(F32)
        totals.append(total.astype(BF16))
    sums = []
    for total in totals:
        low, high = total[:part], total[part:]
        if not sums:
            high = after(high, *came[-1])
        sums.append([send(half, layer=1, zh=a, zl=b) for b, half in enumerate((low, high)) for a in range(2)])
    for chunk, values in zip(CHUNKS, sums):
        piece = with_residual(place, acts, values, chunk)
        late = last = piece
        if values is sums[0]:
            late, last = after(piece, *sums[-1][:2]), after(piece, *sums[-1])
        own = [last, send(piece, y=-1), send(late, y=2), send(last, y=1)]
        pieces += own + [send(p, core=1) for p in own]
    return assembled(place, pieces, acts.shape[2])


def solution(mesh):
    in_specs = (
        P(None, "fsdp", None),
        P(),
        P("fsdp", "section"),
        P("fsdp", "section"),
        P("section", "fsdp"),
    )
    out_specs = P("section", "fsdp", None)
    return jax.shard_map(local, mesh=mesh, in_specs=in_specs, out_specs=out_specs, check_vma=False)
```

```python
import functools

import jax
import jax.numpy as jnp
from jax import lax
from jax.experimental import pallas as pl
from jax.experimental.pallas import tpu as pltpu
from jax.sharding import PartitionSpec as P

AXES = (("layer", 2), ("zh", 2), ("y", 4), ("core", 2), ("x", 4), ("zl", 2))
FIRST = 512
CHUNKS = ((0, 3), (1, 2))
BF16, F32 = jnp.bfloat16, jnp.float32
ROOM = pltpu.CompilerParams(vmem_limit_bytes=40 << 20)


def decode(index):
    place = {}
    for name, size in reversed(AXES):
        place[name] = index % size
        index //= size
    return place


def encode(place):
    index = 0
    for name, size in AXES:
        index = index * size + place[name] % size
    return index


def send(value, **moves):
    pairs = []
    for index in range(256):
        place = decode(index)
        for name, by in moves.items():
            place[name] += by
        pairs.append((index, encode(place)))
    return lax.ppermute(value, ("section", "fsdp"), pairs)


def after(value, *others):
    return lax.optimization_barrier((value, *others))[0]


def dot(a, b):
    return jnp.dot(a, b, preferred_element_type=F32)


def silu(v):
    return v / (1 + jnp.exp(-v))


def turned(value, way):
    pairs = []
    for index in range(256):
        place = decode(index)
        place["x"] += way * (1 - 2 * place["core"])
        pairs.append((index, encode(place)))
    return lax.ppermute(value, ("section", "fsdp"), pairs)


class Ring:
    def __init__(self, depth):
        self.sent, self.depth = [], depth

    def turn(self, value, way):
        if len(self.sent) >= self.depth:
            value = after(value, self.sent[-self.depth])
        self.sent.append(turned(value, way))
        return self.sent[-1]

    def near(self, shard):
        back = self.turn(shard, 1)
        return [shard, self.turn(shard, -1), None, back]

    def far(self, panel, split):
        panel[2] = (self.turn(panel[3][:split], 1), self.turn(panel[1][split:], -1))


def column(place, core, k, b, size):
    slab = lax.rem(place[3] + k + core * (4 - 2 * k), 4)
    return pl.multiple_of((slab * 2 + lax.rem(place[4] + b, 2)) * size, size)


def norm_kernel(place, acts, gains, mine, theirs, normed):
    size = mine.shape[2]
    widened = acts[0].astype(F32)
    meansq = jnp.mean(widened * widened, axis=-1, keepdims=True)
    normed[...] = (widened * lax.rsqrt(meansq + 1e-05) * gains[pl.ds(place[0], 1), :]).astype(BF16)
    for k in range(4):
        mine[k] = normed[:, pl.ds(column(place, place[2], k, 0, size), size)]
        theirs[k] = normed[:, pl.ds(column(place, place[2], k, 1, size), size)]


def normed_slabs(place, acts, gains, slab):
    tokens, width = acts.shape[1:]
    part = tokens // 4
    shape = jax.ShapeDtypeStruct((4, tokens, slab), BF16)
    spec = pl.BlockSpec((4, part, slab), lambda i, place: (0, i, 0))
    return pl.pallas_call(
        norm_kernel,
        grid_spec=pltpu.PrefetchScalarGridSpec(
            num_scalar_prefetch=1,
            grid=(4,),
            in_specs=[
                pl.BlockSpec((1, part, width), lambda i, place: (place[0], lax.rem(place[1] + i, 4), 0)),
                pl.BlockSpec(gains.shape, lambda i, place: (0, 0)),
            ],
            out_specs=[spec, spec],
            scratch_shapes=[pltpu.VMEM((part, width), BF16)],
        ),
        out_shape=[shape, shape],
        compiler_params=ROOM,
    )(place, acts, gains)


def down_kernel(chunk, *refs):
    hidden, panels, (kept, sent) = refs[:8], list(refs[8:-2]), refs[-2:]
    size = panels[0].shape[1]
    part = kept.shape[0] // 2
    first = hidden[0].shape[1]
    for n, k in enumerate(chunk):
        rows = []
        if k == 2:
            for _ in range(2):
                panel = panels.pop(0)
                rows += [panel[:first], panel[first:]]
        else:
            panel = panels.pop(0)
            count = panel.shape[0] // 2
            rows = [panel[:first], panel[first:count], panel[count:count + first], panel[count + first:]]
        columns = slice(n * size, (n + 1) * size)
        for b in range(2):
            product = sum(dot(hidden[4 * b + i][...], rows[i]) for i in range(4))
            kept[b * part:(b + 1) * part, columns] = product[:part]
            for j in range(3):
                sent[j, b * part:(b + 1) * part, columns] = product[(j + 1) * part:(j + 2) * part].astype(BF16)


def down_product(hidden, down, chunk):
    part, size = hidden[0].shape[0] // 2, down[0].shape[1] * len(chunk)
    vmem = pl.BlockSpec(memory_space=pltpu.VMEM)
    flat = []
    for k in chunk:
        flat += down[k] if k == 2 else [down[k]]
    return pl.pallas_call(
        functools.partial(down_kernel, chunk),
        in_specs=[vmem] * (8 + len(flat)),
        out_specs=[vmem, vmem],
        out_shape=[jax.ShapeDtypeStruct((part, size), F32), jax.ShapeDtypeStruct((3, part, size), BF16)],
        compiler_params=ROOM,
    )(*hidden, *flat)


def residual_kernel(chunk, place, acts, *refs):
    out = refs[-1]
    size = refs[0].shape[1] // len(chunk)
    for b in range(2):
        for i, k in enumerate(chunk):
            columns = slice(i * size, (i + 1) * size)
            first = pl.multiple_of(column(place, place[2], k, b, 2 * size) + place[2] * size, size)
            total = acts[0, :, pl.ds(first, size)].astype(F32) + refs[2 * b][:, columns].astype(F32) + refs[2 * b + 1][:, columns].astype(F32)
            first = (len(chunk) * b + i) * size
            out[:, first:first + size] = total.astype(BF16)


def with_residual(place, acts, sums, chunk):
    part, size = sums[0].shape
    block = pl.BlockSpec((part, size), lambda i, place: (0, 0))
    return pl.pallas_call(
        functools.partial(residual_kernel, chunk),
        grid_spec=pltpu.PrefetchScalarGridSpec(
            num_scalar_prefetch=1,
            grid=(1,),
            in_specs=[pl.BlockSpec((1, part, acts.shape[2]), lambda i, place: (1 - place[0], place[1], 0))] + [block] * 4,
            out_specs=pl.BlockSpec((part, 2 * size), lambda i, place: (0, 0)),
        ),
        out_shape=jax.ShapeDtypeStruct((part, 2 * size), BF16),
        compiler_params=ROOM,
    )(place, acts, *sums)


def assembly_kernel(place, *refs):
    out = refs[-1]
    for j in range(4):

        @pl.when(pl.program_id(0) == j)
        def _():
            for c, chunk in enumerate(CHUNKS):
                for i in range(2):
                    piece = refs[8 * c + 4 * i + j]
                    size = piece.shape[1] // (2 * len(chunk))
                    core = lax.rem(place[2] + i, 2)
                    for b in range(2):
                        for n, k in enumerate(chunk):
                            first = pl.multiple_of(column(place, core, k, b, 2 * size) + core * size, size)
                            start = (len(chunk) * b + n) * size
                            out[0, :, pl.ds(first, size)] = piece[:, start:start + size]


def assembled(place, pieces, width):
    part = pieces[0].shape[0]
    return pl.pallas_call(
        assembly_kernel,
        grid_spec=pltpu.PrefetchScalarGridSpec(
            num_scalar_prefetch=1,
            grid=(4,),
            in_specs=[pl.BlockSpec(p.shape, lambda i, place: (0, 0)) for p in pieces],
            out_specs=pl.BlockSpec((1, part, width), lambda i, place: (0, lax.rem(place[1] + i, 4), 0)),
        ),
        out_shape=jax.ShapeDtypeStruct((1, 4 * part, width), BF16),
        compiler_params=ROOM,
    )(place, *pieces)


def local(acts, gains, gate_w, up_w, down_w):
    section, fsdp = lax.axis_index("section"), lax.axis_index("fsdp")
    core = section % 2
    place = jnp.stack([section // 16, section // 2 % 4, core, fsdp // 2, fsdp % 2]).astype(jnp.int32)
    tokens = acts.shape[1]
    slab = gate_w.shape[0]
    part = tokens // 4

    low, high = down_w[:, :slab // 2], down_w[:, slab // 2:]
    down_own = jnp.concatenate([jnp.where(core == 0, low, high), send(jnp.where(core == 0, high, low), core=1)], 0)
    ring = Ring(4)
    gate_panel = ring.near(gate_w)
    first_panel = ring.near(up_w[:, :FIRST])
    ring.far(gate_panel, slab // 2)
    second_panel = ring.near(after(up_w[:, FIRST:], down_own))
    ring.far(first_panel, slab // 2)
    second_panel[1], second_panel[3] = after(second_panel[1], *gate_panel[2]), after(second_panel[3], *gate_panel[2])
    ring.far(second_panel, slab // 2)
    ring.depth = 3
    down_panel = ring.near(after(down_own, *first_panel[2]))

    mine, theirs = normed_slabs(place, acts, gains, slab)
    got = send(theirs, zl=1)

    def partial_sums(panel):
        def product(rows):
            near = sum(dot(rows[k], panel[k]) for k in (0, 1, 3))
            return near + dot(rows[2, :, :slab // 2], panel[2][0]) + dot(rows[2, :, slab // 2:], panel[2][1])

        own, other = product(mine), product(got)
        return own + send(other.astype(BF16), zl=1).astype(F32)

    gate, first, second = partial_sums(gate_panel), partial_sums(first_panel), partial_sums(second_panel)
    kept = [(silu(gate[:, :FIRST]) * first).astype(BF16), (silu(gate[:, FIRST:]) * second).astype(BF16)]
    theirs = [send(h, zl=1) for h in kept]
    near = [send(h, core=1) for h in kept]
    theirs[1] = after(theirs[1], *near)
    hidden = kept + near + theirs + [send(h, core=1) for h in theirs]
    down_panel[1], down_panel[3] = after(down_panel[1], hidden[7]), after(down_panel[3], hidden[7])
    ring.far(down_panel, down_w.shape[0])

    products = [down_product(hidden, down_panel, chunk) for chunk in CHUNKS]
    came = [[send(sent[j - 1], y=j) for j in (1, 3, 2)] for _, sent in products]
    pieces, totals = [], []
    for (total, _), values in zip(products, came):
        total = after(total, products[-1][0])
        for value in values:
            total = total + value.astype(F32)
        totals.append(total.astype(BF16))
    sums = []
    for total in totals:
        low, high = total[:part], total[part:]
        if not sums:
            high = after(high, *came[-1])
        sums.append([send(half, layer=1, zh=a, zl=b) for b, half in enumerate((low, high)) for a in range(2)])
    for chunk, values in zip(CHUNKS, sums):
        piece = with_residual(place, acts, values, chunk)
        late = last = piece
        if values is sums[0]:
            late, last = after(piece, *sums[-1][:2]), after(piece, *sums[-1])
        own = [last, send(piece, y=-1), send(late, y=2), send(last, y=1)]
        pieces += own + [send(p, core=1) for p in own]
    return assembled(place, pieces, acts.shape[2])


def solution(mesh):
    in_specs = (
        P(None, "fsdp", None),
        P(),
        P("fsdp", "section"),
        P("fsdp", "section"),
        P("section", "fsdp"),
    )
    out_specs = P("section", "fsdp", None)
    return jax.shard_map(local, mesh=mesh, in_specs=in_specs, out_specs=out_specs, check_vma=False)
```
